32 devices in a mesh: dp: 4 (over y, x), fsdp: 8 (over z, core).
Axes of the slice: x: 2, y: 2, z: 4, core: 2. Of those that a mesh axis runs over, the one named last changes fastest.
Arguments:
- tokens: bfloat16 [4096, 8192], P('dp', 'fsdp'), may hold values from -72 to 72
- w_query: bfloat16 [8192, 8192], P('dp', 'fsdp'), may hold values from -0.0625 to 0.0625
- w_output: bfloat16 [8192, 8192], P('dp', 'fsdp'), may hold values from -0.5 to 0.5
- neighbor_shard: int32 [64, 2], P('dp'), may hold values from 0 to 3, all different within a row; in each aligned block of 16 rows (0 to 15, 16 to 31, ...) at most 12 rows name the same one
- neighbor_block: int32 [64, 2], P('dp'), may hold values from 0 to 31
- kv_store: bfloat16 [4, 32, 2, 128, 8192], P('dp', None, None, None, 'fsdp'), may hold values from -350 to 350
Outputs:
- cross_output: bfloat16 [4096, 8192], P('dp', 'fsdp')
The draws below stay inside these ranges and needn't reach their ends.
Inputs may be any that keep to these rules, and one draw needn't show every extreme that they name: `neighbor_shard`: the 2 neighbours of one span lie in different shards. Among the 16 spans of one token group no shard is named by more than 12 spans, a bound that some block reaches.
All inputs are finite; a program needn't handle non-finite values.
Results may differ from the reference program's by a relative error of at most 0.0049.
The reference program's roundings to bfloat16 on the way (of `normed`, `queries`, `weights` and `attended`) count: a program that leaves them out, or rounds other values in their place, can miss the bound.
Values may be sent and summed in bfloat16 or wider, within the bound.
No kernel may reach another device: no remote copies, remote signals or barrier semaphores. Data moves between devices by JAX's collectives and lax.ppermute only.
A program may use at most 320 MiB of HBM per device.

```python
import math
import jax
import jax.numpy as jnp
import numpy as np
from jax import lax

D = 8192
HEADS = 64
HEAD_DIM = 128
SPAN = 64
NEIGH = 2
BLOCK = 128
BLK_DEV = 32
HW = 8192
CH_DP = 16
SPANS = 64
TOKENS = 4096
MOST = 12
N_DP = 4


def draw_tokens(key, part):
    first, second, third = jax.random.split(jax.random.fold_in(key, 11), 3)
    row_scale = jnp.exp(jax.random.uniform(second, (TOKENS, 1), jnp.float32, math.log(0.3), math.log(3.0)))
    col_scale = jnp.exp(jax.random.uniform(third, (1, D), jnp.float32, math.log(0.4), math.log(4.0)))
    base = jnp.clip(jax.random.normal(first, (TOKENS, D), jnp.float32), -6.0, 6.0)
    return (base * row_scale * col_scale).astype(jnp.bfloat16)


def draw_kv_store(key, part):
    shape = (N_DP, BLK_DEV, 2, BLOCK, HW)
    first = jax.random.fold_in(jax.random.fold_in(key, 23), 0)
    values = jnp.clip(jax.random.normal(first, shape, jnp.float32), -6.0, 6.0)
    return values.astype(jnp.bfloat16)


def with_ends(values, key, least, top_value):
    spot = [jax.random.randint(jax.random.fold_in(key, axis), (), 0, length) for axis, length in enumerate(values.shape)]
    longest = values.shape.index(max(values.shape))
    beside = spot[:longest] + [(spot[longest] + 1) % values.shape[longest]] + spot[longest + 1:]
    return values.at[tuple(spot)].set(least).at[tuple(beside)].set(top_value)


def block_levels(key, dims, cuts, smallest, high):
    gain = 1.0
    for axis_at, shards_of in cuts:
        steps = jax.random.uniform(jax.random.fold_in(jax.random.fold_in(key, 6), axis_at), (shards_of,), jnp.float32, smallest / len(cuts), high / len(cuts))
        gain = gain * jnp.repeat(jnp.exp(steps), dims[axis_at] // shards_of).reshape((-1,) + (1,) * (len(dims) - 1 - axis_at))
    return gain


def deal_out(rng, own, number, rows, number_of, top, reach, skew):
    ranking = jax.random.permutation(rng, number_of)
    packed, usual = portions_of(number_of, rows * top, reach, skew, True), portions_of(number_of, rows * top, reach, skew, False)
    places = jnp.arange(number_of)

    def named(sizes, rotation):
        used = int((sizes > 0).sum())
        fixed = max(1, used // 4)
        shifted = fixed + (places - fixed + rotation * (used - fixed)) % max(1, number_of - fixed)
        return jnp.zeros((number_of,), jnp.int32).at[ranking[jnp.where(places < fixed, places, shifted)]].set(jnp.asarray(sizes, jnp.int32))

    sizes = jnp.where(number % 4 == 0, named(packed, number // 4), named(usual, number - number // 4 - 1))
    mixed = jax.random.permutation(jax.random.fold_in(own, 3), number_of)
    giver, taker = mixed[0:number_of // 2 * 2:2], mixed[1:number_of // 2 * 2:2]
    margin = jnp.minimum(sizes[giver] - 1, reach - sizes[taker]) // 2
    margin = jnp.where((giver == ranking[0]) | (taker == ranking[0]) | (sizes[taker] == 0), 0, jnp.maximum(margin, 0))
    shifted = jax.random.randint(jax.random.fold_in(own, 4), (number_of // 2,), 0, 1 << 20) % (margin + 1)
    sizes = sizes.at[giver].add(-shifted).at[taker].add(shifted)
    labels = jnp.searchsorted(jnp.cumsum(sizes), jnp.arange(rows * top), side="right").astype(jnp.int32)
    table = labels.reshape(top, rows).T
    table = table[jax.random.permutation(jax.random.fold_in(own, 1), rows)]
    rotation = jax.random.randint(jax.random.fold_in(own, 2), (rows, 1), 0, top)
    return jnp.take_along_axis(table, (jnp.arange(top)[None, :] + rotation) % top, axis=1)


def portions_of(count, total, limit, slope, full):
    loads = [(1 << 20) // math.isqrt(standing ** slope) + 1 for standing in range(1, count + 1)]
    largest = limit if full else min(limit, max(-(-total // count), total * loads[0] // sum(loads)))
    least = 1 if total - largest >= count - 1 else 0
    given, spare = [largest] + [least] * (count - 1), total - largest - least * (count - 1)
    while spare > 0:
        free = [i for i in range(1, count) if given[i] < largest] or [i for i in range(1, count) if given[i] < limit]
        mass, remaining = sum([loads[i] for i in free]), spare
        for i in free:
            addition = min(limit - given[i], max(1, remaining * loads[i] // mass), spare)
            given[i] = given[i] + addition
            spare = spare - addition
    return np.array(given)


def bell_draw(stream_key, extent, spread, most, pieces=(), kind=jnp.bfloat16):
    gain = block_levels(stream_key, extent, pieces, -0.22, 0.18) if pieces else 1.0
    entries = jax.random.normal(stream_key, extent, jnp.float32) * spread * gain
    return jnp.minimum(jnp.maximum(entries, -most), most).astype(kind)


def setup_inputs(seed: int = 0) -> dict:
    splits = jax.random.split(jax.random.key(seed), 7)
    tokens = draw_tokens(jax.random.fold_in(splits[6], 71), 0)
    w_query = bell_draw(splits[1], (D, HW), D ** -0.5, 0.0625, ((0, 4), (1, 8)))
    w_output = bell_draw(splits[2], (HW, D), HEAD_DIM ** -0.5, 0.5, ((0, 4), (1, 8)))
    neighbor_shard_keys = jax.random.split(jax.random.fold_in(splits[3], 1), SPANS // CH_DP)
    neighbor_shard_turns = jax.random.permutation(jax.random.fold_in(splits[3], 3), SPANS // CH_DP)
    neighbor_shard = jax.vmap(lambda own, number: deal_out(jax.random.fold_in(splits[3], 2), own, number, CH_DP, N_DP, NEIGH, MOST, 2))(neighbor_shard_keys, neighbor_shard_turns).reshape((SPANS, NEIGH))
    neighbor_block = with_ends(jax.random.randint(splits[4], (SPANS, NEIGH), 0, BLK_DEV), jax.random.fold_in(splits[4], 1), 0, BLK_DEV - 1).astype(jnp.int32)
    kv_store = draw_kv_store(jax.random.fold_in(splits[6], 71), 0)
    return {"tokens": tokens, "w_query": w_query, "w_output": w_output, "neighbor_shard": neighbor_shard, "neighbor_block": neighbor_block, "kv_store": kv_store}


EPSILON = 1e-05

def reference(tokens, w_query, w_output, neighbor_shard, neighbor_block, kv_store):
    widened = tokens.astype(jnp.float32)
    mean_square = lax.optimization_barrier(jnp.mean(widened * widened, axis=1, keepdims=True))
    normed = (widened * lax.rsqrt(mean_square + EPSILON)).astype(jnp.bfloat16)
    queries = jnp.dot(normed, w_query, preferred_element_type=jnp.float32).astype(jnp.bfloat16)
    span_count = neighbor_shard.shape[0]
    query_grid = queries.reshape(span_count, SPAN, HEADS, HEAD_DIM)

    def one_span(span_id):
        blocks = kv_store[neighbor_shard[span_id], neighbor_block[span_id]]
        key_rows = blocks[:, 0].reshape(NEIGH * BLOCK, HEADS, HEAD_DIM).astype(jnp.float32)
        value_rows = blocks[:, 1].reshape(NEIGH * BLOCK, HEADS, HEAD_DIM).astype(jnp.float32)
        asked = query_grid[span_id].astype(jnp.float32)
        scores = jnp.einsum('qhd,khd->hqk', asked, key_rows) * HEAD_DIM ** (-0.5)
        rounded = jax.nn.softmax(scores, axis=-1).astype(jnp.bfloat16)
        rounded = lax.optimization_barrier(rounded)
        weights = rounded.astype(jnp.float32)
        mixed_heads = jnp.einsum('hqk,khd->qhd', weights, value_rows)
        return mixed_heads.astype(jnp.bfloat16).reshape(SPAN, HEADS * HEAD_DIM)
    attended = lax.map(one_span, jnp.arange(span_count, dtype=jnp.int32))
    attended = attended.reshape(span_count * SPAN, HEADS * HEAD_DIM)
    return jnp.dot(attended, w_output, preferred_element_type=jnp.float32).astype(jnp.bfloat16)
```

```python
import functools

import jax
import jax.numpy as jnp
from jax import lax
from jax.experimental import pallas as pl
from jax.experimental.pallas import tpu as pltpu
from jax.sharding import PartitionSpec as P

HEAD_DIM = 128
NEIGH = 2
CHUNKS = 2

EPSILON = 1e-05


def normalize(features):
    widened = features.astype(jnp.float32)
    mean_square = jnp.mean(widened * widened, axis=1, keepdims=True)
    return (widened * lax.rsqrt(mean_square + EPSILON)).astype(jnp.bfloat16)


def pieces_over_fsdp(piece):
    members = lax.axis_size("fsdp")
    chips = members // 2
    me = lax.axis_index("fsdp")
    chip, core = me // 2, me % 2
    swap = [(i, i ^ 1) for i in range(members)]
    found = []
    for step in range(chips):
        if step == 0:
            here = piece
        else:
            shift = [(z * 2 + c, (z + step) % chips * 2 + c) for z in range(chips) for c in range(2)]
            here = lax.ppermute(piece, "fsdp", shift)
        there = lax.ppermute(here, "fsdp", swap)
        owner = (chip - step + chips) % chips
        found.append((owner * 2 + core, here))
        found.append((owner * 2 + 1 - core, there))
    return found


def pick_kernel(table_ref, stored_ref, *out_refs):
    width = out_refs[0].shape[-1]
    for number, out_ref in enumerate(out_refs):
        out_ref[...] = stored_ref[..., number * width:(number + 1) * width]


def pick_blocks(stored, table, chunks):
    count = table.shape[0]
    _, two, block_size, width = stored.shape
    part = width // chunks
    return pl.pallas_call(
        pick_kernel,
        grid_spec=pltpu.PrefetchScalarGridSpec(
            num_scalar_prefetch=1,
            grid=(count,),
            in_specs=[pl.BlockSpec((1, two, block_size, width), lambda i, t: (t[i], 0, 0, 0))],
            out_specs=[pl.BlockSpec((1, two, block_size, part), lambda i, t: (i, 0, 0, 0))] * chunks,
        ),
        out_shape=[jax.ShapeDtypeStruct((count, two, block_size, part), stored.dtype)] * chunks,
        cost_estimate=pl.CostEstimate(
            flops=0, transcendentals=0, bytes_accessed=count * two * block_size * width * 4
        ),
        name="pick",
    )(table, stored)


def attend_kernel(placed_ref, query_ref, *refs):
    block_refs, out_ref = refs[:-1], refs[-1]
    for head in range(out_ref.shape[1] // HEAD_DIM):
        columns = slice(head * HEAD_DIM, (head + 1) * HEAD_DIM)
        query = query_ref[:, columns]
        keys = jnp.concatenate([ref[0, 0, :, columns] for ref in block_refs], axis=0)
        values = jnp.concatenate([ref[0, 1, :, columns] for ref in block_refs], axis=0)
        scores = lax.dot_general(
            query, keys, (((1,), (1,)), ((), ())), preferred_element_type=jnp.float32
        ) * HEAD_DIM ** (-0.5)
        highest = jnp.max(scores, axis=-1, keepdims=True)
        raised = jnp.exp(scores - highest)
        weights = (raised / jnp.sum(raised, axis=-1, keepdims=True)).astype(jnp.bfloat16)
        mixed = jnp.dot(weights, values, preferred_element_type=jnp.float32)
        out_ref[:, columns] = mixed.astype(jnp.bfloat16)


def attend(queries, blocks, placed, span_count):
    rows, width = queries.shape
    span = rows // span_count
    _, two, block_size, _ = blocks.shape

    def block_spec(j):
        return pl.BlockSpec((1, two, block_size, width), lambda c, p, j=j: (p[c * NEIGH + j], 0, 0, 0))

    return pl.pallas_call(
        attend_kernel,
        grid_spec=pltpu.PrefetchScalarGridSpec(
            num_scalar_prefetch=1,
            grid=(span_count,),
            in_specs=[pl.BlockSpec((span, width), lambda c, p: (c, 0))] + [block_spec(j) for j in range(NEIGH)],
            out_specs=pl.BlockSpec((span, width), lambda c, p: (c, 0)),
        ),
        out_shape=jax.ShapeDtypeStruct((rows, width), jnp.bfloat16),
        cost_estimate=pl.CostEstimate(
            flops=4 * rows * NEIGH * block_size * width,
            transcendentals=rows * NEIGH * block_size * width // HEAD_DIM,
            bytes_accessed=span_count * NEIGH * two * block_size * width * 2 + rows * width * 4,
        ),
        name="attend",
    )(placed, queries, *[blocks] * NEIGH)


def shards(tokens, w_query, w_output, neighbor_shard, neighbor_block, kv_store):
    local_width = w_query.shape[1]
    row_count = tokens.shape[0]
    peers = lax.axis_size("dp")
    members = lax.axis_size("fsdp")
    chunks = CHUNKS if local_width % (CHUNKS * HEAD_DIM) == 0 else 1
    part = local_width // chunks

    w_query_columns = lax.all_gather(w_query, "dp", axis=0, tiled=True)
    w_output_columns = lax.all_gather(w_output, "dp", axis=0, tiled=True)

    span_count = neighbor_shard.shape[0]
    capacity = max(2, 3 * span_count * NEIGH // (2 * peers))
    owners = neighbor_shard.reshape(-1)
    wanted = neighbor_block.reshape(-1)
    owned = (owners[:, None] == jnp.arange(peers, dtype=jnp.int32)[None, :]).astype(jnp.int32)
    earlier = jnp.cumsum(owned, axis=0) - owned
    placed = owners * capacity + jnp.sum(earlier * owned, axis=1)
    matches = placed[:, None] == jnp.arange(peers * capacity, dtype=jnp.int32)[None, :]
    table = jnp.sum(jnp.where(matches, wanted[:, None], 0), axis=0).reshape(peers, capacity)
    asked = lax.all_to_all(table, "dp", split_axis=0, concat_axis=0, tiled=True)
    picked = pick_blocks(kv_store[0], asked.reshape(-1), chunks)
    replies = [
        lax.all_to_all(
            blocks.reshape((peers, capacity) + blocks.shape[1:]), "dp", split_axis=0, concat_axis=0, tiled=True
        ).reshape(blocks.shape)
        for blocks in picked
    ]

    width = tokens.shape[1]
    gathered = jnp.zeros((row_count, members * width), tokens.dtype)
    for owner, piece in pieces_over_fsdp(tokens):
        gathered = lax.dynamic_update_slice(gathered, piece, (0, owner * width))
    normed = normalize(gathered)
    queries = jnp.dot(normed, w_query_columns, preferred_element_type=jnp.float32).astype(jnp.bfloat16)

    attended = jnp.zeros((row_count, members * local_width), jnp.bfloat16)
    for chunk in range(chunks):
        mixed = attend(queries[:, chunk * part:(chunk + 1) * part], replies[chunk], placed, span_count)
        for owner, piece in pieces_over_fsdp(mixed):
            attended = lax.dynamic_update_slice(attended, piece, (0, owner * local_width + chunk * part))
    summed = jnp.dot(attended, w_output_columns, preferred_element_type=jnp.float32)
    return summed.astype(jnp.bfloat16)


def solution(mesh):
    in_specs = (
        P("dp", "fsdp"),
        P("dp", "fsdp"),
        P("dp", "fsdp"),
        P("dp", None),
        P("dp", None),
        P("dp", None, None, None, "fsdp"),
    )
    out_specs = P("dp", "fsdp")
    return jax.shard_map(shards, mesh=mesh, in_specs=in_specs, out_specs=out_specs, check_vma=False)
```

```python
import functools

import jax
import jax.numpy as jnp
from jax import lax
from jax.experimental import pallas as pl
from jax.experimental.pallas import tpu as pltpu
from jax.sharding import PartitionSpec as P

HEAD_DIM = 128
NEIGH = 2
AXES = 2
LANES = 128
ABSENT = -1e30

EPSILON = 1e-05


def normalize(features):
    widened = features.astype(jnp.float32)
    mean_square = jnp.mean(widened * widened, axis=1, keepdims=True)
    return (widened * lax.rsqrt(mean_square + EPSILON)).astype(jnp.bfloat16)


def over_dp(value, bit):
    return lax.ppermute(value, "dp", [(i, i ^ bit) for i in range(lax.axis_size("dp"))])


def pieces_over_fsdp(piece):
    members = lax.axis_size("fsdp")
    chips = members // 2
    if chips != 4:
        whole = lax.all_gather(piece, "fsdp", axis=0)
        return [(i, whole[i]) for i in range(members)]
    me = lax.axis_index("fsdp")
    chip, core = me // 2, me % 2

    def chip_pairs(pairs):
        return [(a * 2 + c, b * 2 + c) for a, b in pairs for c in range(2)]

    back1 = lax.ppermute(piece, "fsdp", chip_pairs([(0, 1), (1, 2), (2, 3)]))
    back3 = lax.ppermute(piece, "fsdp", chip_pairs([(1, 0), (2, 1), (3, 2)]))
    back2 = lax.ppermute(piece, "fsdp", chip_pairs([(0, 2), (1, 3), (2, 0), (3, 1)]))
    ends = lax.ppermute(back2, "fsdp", chip_pairs([(2, 3), (1, 0)]))
    back1 = jnp.where(chip == 0, ends, back1)
    back3 = jnp.where(chip == 3, ends, back3)
    found = []
    for step, here in enumerate((piece, back1, back2, back3)):
        there = lax.ppermute(here, "fsdp", [(i, i ^ 1) for i in range(members)])
        owner = (chip + 4 - step) % 4
        found.append((owner * 2 + core, here))
        found.append((owner * 2 + 1 - core, there))
    return found


def pick_kernel(first_ref, second_ref, *refs):
    for axis in range(AXES):
        refs[AXES + axis][...] = refs[axis][...]


def pick_blocks(stored, tables, step, part):
    count = tables[0].shape[0]
    _, two, block_size, _ = stored.shape
    shape = (1, two, block_size, part)
    return pl.pallas_call(
        pick_kernel,
        grid_spec=pltpu.PrefetchScalarGridSpec(
            num_scalar_prefetch=AXES,
            grid=(count,),
            in_specs=[
                pl.BlockSpec(shape, lambda i, *t, axis=axis: (t[axis][i], 0, 0, step * AXES + axis))
                for axis in range(AXES)
            ],
            out_specs=[pl.BlockSpec(shape, lambda i, *t: (i, 0, 0, 0))] * AXES,
        ),
        out_shape=[jax.ShapeDtypeStruct((count,) + shape[1:], stored.dtype)] * AXES,
        cost_estimate=pl.CostEstimate(
            flops=0, transcendentals=0, bytes_accessed=count * two * block_size * part * 4 * AXES
        ),
        name="pick",
    )(*tables, *[stored] * AXES)


def scores_of(query, keys, present):
    scores = lax.dot_general(
        query, keys, (((1,), (1,)), ((), ())), preferred_element_type=jnp.float32
    ) * HEAD_DIM ** (-0.5)
    return jnp.where(present == 1, scores, ABSENT)


def head_columns(head):
    return slice(head * HEAD_DIM, (head + 1) * HEAD_DIM)


def presence(index_refs, axis):
    entry = pl.program_id(0) * pl.num_programs(1) + pl.program_id(1)
    here_at, far_at = index_refs[axis * 2], index_refs[axis * 2 + 1]
    return here_at[entry] >= 0, far_at[entry] >= 0


def all_scores(index_refs, query_refs, here_refs, far_refs):
    found = []
    for axis in range(AXES):
        has_here, has_far = presence(index_refs, axis)
        for head in range(query_refs[axis].shape[1] // HEAD_DIM):
            columns = head_columns(head)
            query = query_refs[axis][:, columns]
            found.append((
                axis,
                head,
                scores_of(query, here_refs[axis][0, 0, :, columns], has_here.astype(jnp.int32)),
                scores_of(query, far_refs[axis][0, 0, :, columns], has_far.astype(jnp.int32)),
            ))
    return found


def stats_kernel(*refs):
    index_refs, refs = refs[:2 * AXES], refs[2 * AXES:]
    query_refs, here_refs, far_refs, out_refs = (refs[i * AXES:(i + 1) * AXES] for i in range(4))
    span = pl.program_id(1)

    @pl.when(span == 0)
    def _():
        for out_ref in out_refs:
            out_ref[...] = jnp.zeros_like(out_ref)

    found = all_scores(index_refs, query_refs, here_refs, far_refs)
    highest = [jnp.max(jnp.maximum(here, far), axis=-1, keepdims=True) for _, _, here, far in found]
    totals = [
        jnp.sum(jnp.exp(here - top) + jnp.exp(far - top), axis=-1, keepdims=True)
        for (_, _, here, far), top in zip(found, highest)
    ]
    heads = len(found) // AXES
    lane = lax.broadcasted_iota(jnp.int32, out_refs[0].shape[1:], 1)
    for axis in range(AXES):
        kept = out_refs[axis][0]
        for head in range(heads):
            at = (span * heads + head) * 2
            kept = jnp.where(lane == at, highest[axis * heads + head], kept)
            kept = jnp.where(lane == at + 1, totals[axis * heads + head], kept)
        out_refs[axis][0] = kept


def mix_kernel(*refs):
    index_refs, refs = refs[:2 * AXES], refs[2 * AXES:]
    query_refs, here_refs, far_refs, mine_refs, their_refs, out_refs = (
        refs[i * AXES:(i + 1) * AXES] for i in range(6)
    )
    span = pl.program_id(1)
    found = all_scores(index_refs, query_refs, here_refs, far_refs)
    heads = len(found) // AXES
    lane = lax.broadcasted_iota(jnp.int32, mine_refs[0].shape[1:], 1)

    def column(stats, at):
        return jnp.sum(jnp.where(lane == at, stats, 0.0), axis=-1, keepdims=True)

    scales = []
    for axis in range(AXES):
        mine, theirs = mine_refs[axis][0], their_refs[axis][0]
        for head in range(heads):
            at = (span * heads + head) * 2
            my_top, their_top = column(mine, at), column(theirs, at)
            top = jnp.maximum(my_top, their_top)
            total = column(mine, at + 1) * jnp.exp(my_top - top) + column(theirs, at + 1) * jnp.exp(their_top - top)
            scales.append((top, 1.0 / total))
    weights = [
        jnp.concatenate([jnp.exp(here - top) * scale, jnp.exp(far - top) * scale], axis=1).astype(jnp.bfloat16)
        for (_, _, here, far), (top, scale) in zip(found, scales)
    ]
    for (axis, head, _, _), weight in zip(found, weights):
        columns = head_columns(head)
        values = jnp.concatenate([here_refs[axis][0, 1, :, columns], far_refs[axis][0, 1, :, columns]], axis=0)
        out_refs[axis][0, :, columns] = jnp.dot(weight, values, preferred_element_type=jnp.float32)


def span_call(kernel, indices, queries, stored, received, stats, step, part, spans, planes, out_block, out_index, out_shape, name):
    rows = queries[0].shape[0]
    span = rows // (2 * spans)
    block_size = stored.shape[2]

    def at(c, i):
        return c * spans + i

    in_specs = [pl.BlockSpec((span, part), lambda c, i, *t: (at(c, i), 0))] * AXES
    in_specs += [
        pl.BlockSpec(
            (1, planes, block_size, part),
            lambda c, i, *t, axis=axis: (jnp.maximum(t[axis * 2][at(c, i)], 0), 0, 0, step * AXES + axis),
        )
        for axis in range(AXES)
    ]
    in_specs += [
        pl.BlockSpec(
            (1, planes, block_size, part),
            lambda c, i, *t, axis=axis: (jnp.maximum(t[axis * 2 + 1][at(c, i)], 0), 0, 0, 0),
        )
        for axis in range(AXES)
    ]
    if stats:
        in_specs += [pl.BlockSpec((1, span, LANES), lambda c, i, *t: (c, 0, 0))] * AXES
        in_specs += [pl.BlockSpec((1, span, LANES), lambda c, i, *t: (1 - c, 0, 0))] * AXES
    return pl.pallas_call(
        kernel,
        grid_spec=pltpu.PrefetchScalarGridSpec(
            num_scalar_prefetch=2 * AXES,
            grid=(2, spans),
            in_specs=in_specs,
            out_specs=[pl.BlockSpec(out_block, out_index)] * AXES,
        ),
        out_shape=[jax.ShapeDtypeStruct(out_shape, jnp.float32)] * AXES,
        cost_estimate=pl.CostEstimate(
            flops=4 * rows * NEIGH * block_size * part * AXES * planes,
            transcendentals=rows * NEIGH * block_size * part * AXES // HEAD_DIM,
            bytes_accessed=2 * spans * NEIGH * planes * block_size * part * 2 * AXES,
        ),
        name=name,
    )(*indices, *queries, *[stored] * AXES, *received, *stats)


def exchange_tables(neighbor_shard, neighbor_block, capacity):
    me = lax.axis_index("dp")
    both = jnp.concatenate([neighbor_shard, neighbor_block], axis=1)
    groups = jnp.stack([both] + [over_dp(both, bit) for bit in (1, 2, 3)])
    spans = both.shape[0]
    owners = groups[:, :, :NEIGH].reshape(4, spans * NEIGH)
    wanted = groups[:, :, NEIGH:].reshape(4, spans * NEIGH)
    order = jnp.arange(spans * NEIGH, dtype=jnp.int32)
    same = (owners[:, :, None] == owners[:, None, :]) & (order[None, None, :] < order[None, :, None])
    rank = jnp.sum(same.astype(jnp.int32), axis=2)
    slots = jnp.arange(capacity, dtype=jnp.int32)
    hit = (owners == me)[:, :, None] & (rank[:, :, None] == slots[None, None, :])
    table = jnp.sum(jnp.where(hit, wanted[:, :, None], 0), axis=1)
    sends, places = [], []
    for axis in range(AXES):
        near = 1 << axis
        partner = 3 ^ near
        sends.append(jnp.concatenate([table[near], table[3]]))
        here, far = [], []
        for position, group in enumerate((0, partner)):
            mine = (owners[group] == me).reshape(spans, NEIGH)
            other = (owners[group] == me ^ near).reshape(spans, NEIGH)
            block = wanted[group].reshape(spans, NEIGH)
            slot = rank[group].reshape(spans, NEIGH) + position * capacity
            here.append(jnp.max(jnp.where(mine, block, -1), axis=1))
            far.append(jnp.max(jnp.where(other, slot, -1), axis=1))
        places += [jnp.concatenate(here), jnp.concatenate(far)]
    return sends, places


def shards(tokens, w_query, w_output, neighbor_shard, neighbor_block, kv_store):
    local_width = w_query.shape[1]
    row_count, width = tokens.shape
    peers = lax.axis_size("dp")
    members = lax.axis_size("fsdp")
    passes = 2 if local_width % (2 * AXES * HEAD_DIM) == 0 else 1
    part = local_width // (passes * AXES)
    span_count = neighbor_shard.shape[0]
    span = row_count // span_count
    capacity = max(2, 3 * span_count * NEIGH // (2 * peers))

    w_query_columns = lax.all_gather(w_query, "dp", axis=0, tiled=True)

    sends, places = exchange_tables(neighbor_shard, neighbor_block, capacity)
    stored = kv_store[0]
    received = []
    for step in range(passes):
        picked = pick_blocks(stored, sends, step, part)
        received.append([over_dp(picked[axis], 1 << axis) for axis in range(AXES)])

    w_output, _ = lax.optimization_barrier((w_output, received[-1]))
    w_output_columns = lax.all_gather(w_output, "dp", axis=0, tiled=True)

    gathered = jnp.zeros((row_count, members * width), tokens.dtype)
    for owner, piece in pieces_over_fsdp(tokens):
        gathered = lax.dynamic_update_slice(gathered, piece, (0, owner * width))
    normed = normalize(gathered)
    queries = jnp.dot(normed, w_query_columns, preferred_element_type=jnp.float32).astype(jnp.bfloat16)

    attended = jnp.zeros((row_count, members * local_width), jnp.bfloat16)
    for step in range(passes):
        asked = []
        for axis in range(AXES):
            start = (step * AXES + axis) * part
            own = queries[:, start:start + part]
            asked.append(jnp.concatenate([own, over_dp(own, 3 ^ (1 << axis))], axis=0))
        common = dict(step=step, part=part, spans=span_count)
        mine = span_call(
            stats_kernel, places, asked, stored, received[step], [], planes=1,
            out_block=(1, span, LANES), out_index=lambda c, i, *t: (c, 0, 0),
            out_shape=(2, span, LANES), name="stats", **common,
        )
        theirs = [over_dp(mine[axis], 3 ^ (1 << axis)) for axis in range(AXES)]
        partial = span_call(
            mix_kernel, places, asked, stored, received[step], list(mine) + theirs, planes=2,
            out_block=(1, span, part), out_index=lambda c, i, *t: (c, i, 0),
            out_shape=(2, row_count, part), name="mix", **common,
        )
        mixed = jnp.concatenate(
            [
                (partial[axis][0] + over_dp(partial[axis][1], 3 ^ (1 << axis))).astype(jnp.bfloat16)
                for axis in range(AXES)
            ],
            axis=1,
        )
        for owner, piece in pieces_over_fsdp(mixed):
            start = owner * local_width + step * AXES * part
            attended = lax.dynamic_update_slice(attended, piece, (0, start))
    summed = jnp.dot(attended, w_output_columns, preferred_element_type=jnp.float32)
    return summed.astype(jnp.bfloat16)


def solution(mesh):
    in_specs = (
        P("dp", "fsdp"),
        P("dp", "fsdp"),
        P("dp", "fsdp"),
        P("dp", None),
        P("dp", None),
        P("dp", None, None, None, "fsdp"),
    )
    out_specs = P("dp", "fsdp")
    return jax.shard_map(shards, mesh=mesh, in_specs=in_specs, out_specs=out_specs, check_vma=False)
```

```python
import functools

import jax
import jax.numpy as jnp
from jax import lax
from jax.experimental import pallas as pl
from jax.experimental.pallas import tpu as pltpu
from jax.sharding import PartitionSpec as P


HEAD_DIM = 128
NEIGH = 2
AXES = 2
LANES = 128
ABSENT = -1e30

EPSILON = 1e-05


def normalize(features):
    widened = features.astype(jnp.float32)
    mean_square = jnp.mean(widened * widened, axis=1, keepdims=True)
    return (widened * lax.rsqrt(mean_square + EPSILON)).astype(jnp.bfloat16)


def over_dp(value, bit):
    return lax.ppermute(value, "dp", [(i, i ^ bit) for i in range(lax.axis_size("dp"))])


def pieces_over_fsdp(piece):
    members = lax.axis_size("fsdp")
    chips = members // 2
    if chips != 4:
        whole = lax.all_gather(piece, "fsdp", axis=0)
        return [(i, whole[i]) for i in range(members)]
    me = lax.axis_index("fsdp")
    chip, core = me // 2, me % 2

    def chip_pairs(pairs):
        return [(a * 2 + c, b * 2 + c) for a, b in pairs for c in range(2)]

    back1 = lax.ppermute(piece, "fsdp", chip_pairs([(0, 1), (1, 2), (2, 3)]))
    back3 = lax.ppermute(piece, "fsdp", chip_pairs([(1, 0), (2, 1), (3, 2)]))
    back2 = lax.ppermute(piece, "fsdp", chip_pairs([(0, 2), (1, 3), (2, 0), (3, 1)]))
    ends = lax.ppermute(back2, "fsdp", chip_pairs([(2, 3), (1, 0)]))
    back1 = jnp.where(chip == 0, ends, back1)
    back3 = jnp.where(chip == 3, ends, back3)
    found = []
    for step, here in enumerate((piece, back1, back2, back3)):
        there = lax.ppermute(here, "fsdp", [(i, i ^ 1) for i in range(members)])
        owner = (chip + 4 - step) % 4
        found.append((owner * 2 + core, here))
        found.append((owner * 2 + 1 - core, there))
    return found


def pick_kernel(first_ref, second_ref, *refs):
    for axis in range(AXES):
        refs[AXES + axis][...] = refs[axis][...]


def pick_blocks(stored, tables, step, part):
    count = tables[0].shape[0]
    _, two, block_size, _ = stored.shape
    shape = (1, two, block_size, part)
    return pl.pallas_call(
        pick_kernel,
        grid_spec=pltpu.PrefetchScalarGridSpec(
            num_scalar_prefetch=AXES,
            grid=(count,),
            in_specs=[
                pl.BlockSpec(shape, lambda i, *t, axis=axis: (t[axis][i], 0, 0, step * AXES + axis))
                for axis in range(AXES)
            ],
            out_specs=[pl.BlockSpec(shape, lambda i, *t: (i, 0, 0, 0))] * AXES,
        ),
        out_shape=[jax.ShapeDtypeStruct((count,) + shape[1:], stored.dtype)] * AXES,
        cost_estimate=pl.CostEstimate(
            flops=0, transcendentals=0, bytes_accessed=count * two * block_size * part * 4 * AXES
        ),
        name="pick",
    )(*tables, *[stored] * AXES)


def send_blocks(picked, after):
    picked, _ = lax.optimization_barrier((picked, after))
    return [over_dp(picked[axis], 1 << axis) for axis in range(AXES)]


def scores_of(query, keys, present):
    scores = lax.dot_general(
        query, keys, (((1,), (1,)), ((), ())), preferred_element_type=jnp.float32
    ) * HEAD_DIM ** (-0.5)
    return jnp.where(present, scores, ABSENT)


def head_columns(head):
    return slice(head * HEAD_DIM, (head + 1) * HEAD_DIM)


def span_units(index_refs, query_refs, here_ref, far_refs, spans, span, first, together):
    per_step = query_refs[0].shape[0] // span
    part = query_refs[0].shape[1]
    units = []
    for local in (first + number for number in range(together)):
        in_group = pl.program_id(1) * per_step + local
        entry = pl.program_id(0) * spans + in_group
        rows = pl.ds(pl.multiple_of(local * span, span), span)
        for axis in range(AXES):
            here_at, far_at = index_refs[axis * 2][entry], index_refs[axis * 2 + 1][entry]
            here_block, far_block = jnp.maximum(here_at, 0), jnp.maximum(far_at, 0)
            for head in range(part // HEAD_DIM):
                columns = head_columns(head)
                here_columns = head_columns(axis * (part // HEAD_DIM) + head)
                query = query_refs[axis][rows, columns]
                here = scores_of(query, here_ref[here_block, 0, :, here_columns], here_at >= 0)
                far = scores_of(query, far_refs[axis][far_block, 0, :, columns], far_at >= 0)
                lane = (in_group * (part // HEAD_DIM) + head) * 2
                units.append((axis, rows, columns, here_block, here_columns, far_block, lane, here, far))
    return units


def stats_kernel(spans, span, together, *refs):
    index_refs, refs = refs[:2 * AXES], refs[2 * AXES:]
    query_refs, here_ref, far_refs, out_refs = refs[:AXES], refs[AXES], refs[AXES + 1:2 * AXES + 1], refs[2 * AXES + 1:]
    per_step = query_refs[0].shape[0] // span

    @pl.when(pl.program_id(1) == 0)
    def _():
        for out_ref in out_refs:
            out_ref[...] = jnp.zeros_like(out_ref)

    lanes = lax.broadcasted_iota(jnp.int32, out_refs[0].shape[1:], 1)

    def some(turn, carry):
        units = span_units(index_refs, query_refs, here_ref, far_refs, spans, span, turn * together, together)
        tops = [jnp.max(jnp.maximum(unit[-2], unit[-1]), axis=-1, keepdims=True) for unit in units]
        totals = [
            jnp.sum(jnp.exp(unit[-2] - top) + jnp.exp(unit[-1] - top), axis=-1, keepdims=True)
            for unit, top in zip(units, tops)
        ]
        for axis in range(AXES):
            kept = out_refs[axis][0]
            for unit, top, total in zip(units, tops, totals):
                if unit[0] == axis:
                    kept = jnp.where(lanes == unit[6], top, kept)
                    kept = jnp.where(lanes == unit[6] + 1, total, kept)
            out_refs[axis][0] = kept
        return carry

    lax.fori_loop(0, per_step // together, some, 0)


def mix_kernel(spans, span, together, *refs):
    index_refs, refs = refs[:2 * AXES], refs[2 * AXES:]
    query_refs, here_ref, far_refs, refs = refs[:AXES], refs[AXES], refs[AXES + 1:2 * AXES + 1], refs[2 * AXES + 1:]
    mine_refs, their_refs, keep_refs, send_refs = (refs[i * AXES:(i + 1) * AXES] for i in range(4))
    per_step = query_refs[0].shape[0] // span
    lanes = lax.broadcasted_iota(jnp.int32, mine_refs[0].shape[1:], 1)

    def column(stats, at):
        return jnp.sum(jnp.where(lanes == at, stats, 0.0), axis=-1, keepdims=True)

    def some(out_refs, turn, carry):
        units = span_units(index_refs, query_refs, here_ref, far_refs, spans, span, turn * together, together)
        scales = []
        for unit in units:
            mine, theirs, at = mine_refs[unit[0]][0], their_refs[unit[0]][0], unit[6]
            my_top, their_top = column(mine, at), column(theirs, at)
            top = jnp.maximum(my_top, their_top)
            total = column(mine, at + 1) * jnp.exp(my_top - top) + column(theirs, at + 1) * jnp.exp(their_top - top)
            scales.append((top, 1.0 / total))
        weights = [
            jnp.concatenate(
                [jnp.exp(unit[-2] - top) * scale, jnp.exp(unit[-1] - top) * scale], axis=1
            ).astype(jnp.bfloat16)
            for unit, (top, scale) in zip(units, scales)
        ]
        for (axis, rows, columns, here_block, here_columns, far_block, _, _, _), weight in zip(units, weights):
            values = jnp.concatenate(
                [here_ref[here_block, 1, :, here_columns], far_refs[axis][far_block, 1, :, columns]], axis=0
            )
            out_refs[axis][rows, columns] = jnp.dot(weight, values, preferred_element_type=jnp.float32)
        return carry

    for group, out_refs in enumerate((keep_refs, send_refs)):
        @pl.when(pl.program_id(0) == group)
        def _(out_refs=out_refs):
            lax.fori_loop(0, per_step // together, functools.partial(some, out_refs), 0)


def span_call(kernel, indices, queries, stored, received, stats, step, part, spans, planes):
    rows = queries[0].shape[0] // 2
    span = rows // spans
    count, _, block_size, _ = stored.shape
    per_step = 8 if spans % 8 == 0 else spans
    steps = spans // per_step
    together = 2 if per_step % 2 == 0 else 1
    step_rows = per_step * span

    in_specs = [pl.BlockSpec((step_rows, part), lambda c, i, *t: (c * steps + i, step))] * AXES
    in_specs += [pl.BlockSpec((count, planes, block_size, AXES * part), lambda c, i, *t: (0, 0, 0, step))]
    in_specs += [
        pl.BlockSpec((received[0].shape[0], planes, block_size, part), lambda c, i, *t: (0, 0, 0, 0))
    ] * AXES
    if stats:
        in_specs += [pl.BlockSpec((1, span, LANES), lambda c, i, *t: (c, 0, 0))] * AXES
        in_specs += [pl.BlockSpec((1, span, LANES), lambda c, i, *t: (1 - c, 0, 0))] * AXES
        out_specs = [pl.BlockSpec((step_rows, part), lambda c, i, *t: (jnp.where(c == 0, i, steps - 1), 0))] * AXES
        out_specs += [pl.BlockSpec((step_rows, part), lambda c, i, *t: (jnp.where(c == 0, 0, i), 0))] * AXES
        out_shape = [jax.ShapeDtypeStruct((rows, part), jnp.float32)] * (2 * AXES)
    else:
        out_specs = [pl.BlockSpec((1, span, LANES), lambda c, i, *t: (c, 0, 0))] * AXES
        out_shape = [jax.ShapeDtypeStruct((2, span, LANES), jnp.float32)] * AXES
    return pl.pallas_call(
        functools.partial(kernel, spans, span, together),
        grid_spec=pltpu.PrefetchScalarGridSpec(
            num_scalar_prefetch=2 * AXES,
            grid=(2, steps),
            in_specs=in_specs,
            out_specs=out_specs,
        ),
        out_shape=out_shape,
        cost_estimate=pl.CostEstimate(
            flops=8 * rows * NEIGH * block_size * part * AXES * planes,
            transcendentals=2 * rows * NEIGH * block_size * part * AXES // HEAD_DIM,
            bytes_accessed=(count + received[0].shape[0]) * planes * block_size * part * 2 * AXES,
        ),
        name="mix" if stats else "stats",
    )(*indices, *queries, stored, *received, *stats)


def exchange_tables(neighbor_shard, neighbor_block, capacity):
    me = lax.axis_index("dp")
    both = jnp.concatenate([neighbor_shard, neighbor_block], axis=1)
    groups = jnp.stack([both] + [over_dp(both, bit) for bit in (1, 2, 3)])
    spans = both.shape[0]
    owners = groups[:, :, :NEIGH].reshape(4, spans * NEIGH)
    wanted = groups[:, :, NEIGH:].reshape(4, spans * NEIGH)
    order = jnp.arange(spans * NEIGH, dtype=jnp.int32)
    same = (owners[:, :, None] == owners[:, None, :]) & (order[None, None, :] < order[None, :, None])
    rank = jnp.sum(same.astype(jnp.int32), axis=2)
    slots = jnp.arange(capacity, dtype=jnp.int32)
    hit = (owners == me)[:, :, None] & (rank[:, :, None] == slots[None, None, :])
    table = jnp.sum(jnp.where(hit, wanted[:, :, None], 0), axis=1)
    sends, places = [], []
    for axis in range(AXES):
        near = 1 << axis
        partner = 3 ^ near
        sends.append(jnp.concatenate([table[near], table[3]]))
        here, far = [], []
        for position, group in enumerate((0, partner)):
            mine = (owners[group] == me).reshape(spans, NEIGH)
            other = (owners[group] == me ^ near).reshape(spans, NEIGH)
            block = wanted[group].reshape(spans, NEIGH)
            slot = rank[group].reshape(spans, NEIGH) + position * capacity
            here.append(jnp.max(jnp.where(mine, block, -1), axis=1))
            far.append(jnp.max(jnp.where(other, slot, -1), axis=1))
        places += [jnp.concatenate(here), jnp.concatenate(far)]
    return sends, places


def work(tokens, w_query, w_output, neighbor_shard, neighbor_block, kv_store):
    local_width = w_query.shape[1]
    row_count, width = tokens.shape
    peers = lax.axis_size("dp")
    members = lax.axis_size("fsdp")
    passes = 2 if local_width % (2 * AXES * HEAD_DIM) == 0 else 1
    part = local_width // (passes * AXES)
    span_count = neighbor_shard.shape[0]
    capacity = max(2, 3 * span_count * NEIGH // (2 * peers))

    w_query_columns = lax.all_gather(w_query, "dp", axis=0, tiled=True)

    sends, places = exchange_tables(neighbor_shard, neighbor_block, capacity)
    stored = kv_store[0]
    picked = [pick_blocks(stored, sends, step, part) for step in range(passes)]

    pieces = pieces_over_fsdp(tokens)
    received = [send_blocks(picked[0], pieces[-1][1])]

    gathered = jnp.zeros((row_count, members * width), tokens.dtype)
    for owner, piece in pieces:
        gathered = lax.dynamic_update_slice(gathered, piece, (0, owner * width))
    normed = normalize(gathered)
    queries = jnp.dot(normed, w_query_columns, preferred_element_type=jnp.float32).astype(jnp.bfloat16)

    asked = []
    for axis in range(AXES):
        starts = [(step * AXES + axis) * part for step in range(passes)]
        own = jnp.concatenate([queries[:, start:start + part] for start in starts], axis=1)
        asked.append(jnp.concatenate([own, over_dp(own, 3 ^ (1 << axis))], axis=0))
    for step in range(1, passes):
        received.append(send_blocks(picked[step], asked[0]))

    attended = jnp.zeros((row_count, members * local_width), jnp.bfloat16)
    for step in range(passes):
        common = dict(step=step, part=part, spans=span_count)
        mine = span_call(
            stats_kernel, places, asked, stored, received[step], [], planes=1, **common
        )
        theirs = [over_dp(mine[axis], 3 ^ (1 << axis)) for axis in range(AXES)]
        partial = span_call(mix_kernel, places, asked, stored, received[step], list(mine) + theirs, planes=2, **common)
        if step == 0:
            w_output, _ = lax.optimization_barrier((w_output, partial))
            w_output_columns = lax.all_gather(w_output, "dp", axis=0, tiled=True)
        others = [over_dp(partial[AXES + axis], 3 ^ (1 << axis)) for axis in range(AXES)]
        mixed = jnp.concatenate(
            [(partial[axis] + others[axis]).astype(jnp.bfloat16) for axis in range(AXES)], axis=1
        )
        pieces = pieces_over_fsdp(mixed)
        for owner, piece in pieces:
            start = owner * local_width + step * AXES * part
            attended = lax.dynamic_update_slice(attended, piece, (0, start))
    summed = jnp.dot(attended, w_output_columns, preferred_element_type=jnp.float32)
    return summed.astype(jnp.bfloat16)


def solution(mesh):
    in_specs = (
        P("dp", "fsdp"),
        P("dp", "fsdp"),
        P("dp", "fsdp"),
        P("dp", None),
        P("dp", None),
        P("dp", None, None, None, "fsdp"),
    )
    out_specs = P("dp", "fsdp")
    return jax.shard_map(work, mesh=mesh, in_specs=in_specs, out_specs=out_specs, check_vma=False)
```

```python
import functools

import jax
import jax.numpy as jnp
from jax import lax
from jax.experimental import pallas as pl
from jax.experimental.pallas import tpu as pltpu
from jax.sharding import PartitionSpec as P


HEAD_DIM = 128
NEIGH = 2
AXES = 2
LANES = 128
ABSENT = -1e30

EPSILON = 1e-05


def normalize(features):
    widened = features.astype(jnp.float32)
    mean_square = jnp.mean(widened * widened, axis=1, keepdims=True)
    return (widened * lax.rsqrt(mean_square + EPSILON)).astype(jnp.bfloat16)


def over_dp(value, bit):
    return lax.ppermute(value, "dp", [(i, i ^ bit) for i in range(lax.axis_size("dp"))])


def pieces_over_fsdp(piece):
    members = lax.axis_size("fsdp")
    chips = members // 2
    if chips != 4:
        whole = lax.all_gather(piece, "fsdp", axis=0)
        return [(i, whole[i]) for i in range(members)]
    me = lax.axis_index("fsdp")
    chip, core = me // 2, me % 2

    def chip_pairs(pairs):
        return [(a * 2 + c, b * 2 + c) for a, b in pairs for c in range(2)]

    def swap(value):
        return lax.ppermute(value, "fsdp", [(i, i ^ 1) for i in range(members)])

    back2 = lax.ppermute(piece, "fsdp", chip_pairs([(0, 2), (1, 3), (2, 0), (3, 1)]))
    back1 = lax.ppermute(piece, "fsdp", chip_pairs([(0, 1), (1, 2), (2, 3)]))
    back3 = lax.ppermute(piece, "fsdp", chip_pairs([(1, 0), (2, 1), (3, 2)]))
    own_there = swap(piece)
    ends = lax.ppermute(back2, "fsdp", chip_pairs([(2, 3), (1, 0)]))
    there1, there2, there3 = swap(back1), swap(back2), swap(back3)
    ends_there = lax.ppermute(ends, "fsdp", [(0, 1), (1, 0), (6, 7), (7, 6)])
    found = []
    for step, (here, there) in enumerate((
        (piece, own_there),
        (jnp.where(chip == 0, ends, back1), jnp.where(chip == 0, ends_there, there1)),
        (back2, there2),
        (jnp.where(chip == 3, ends, back3), jnp.where(chip == 3, ends_there, there3)),
    )):
        owner = (chip + 4 - step) % 4
        found.append((owner * 2 + core, here))
        found.append((owner * 2 + 1 - core, there))
    return found


def pick_kernel(first_ref, second_ref, *refs):
    for axis in range(AXES):
        for plane in range(2):
            refs[AXES + axis * 2 + plane][...] = refs[axis][:, plane]


def pick_blocks(stored, tables, step, part):
    count = tables[0].shape[0]
    _, two, block_size, _ = stored.shape
    return pl.pallas_call(
        pick_kernel,
        grid_spec=pltpu.PrefetchScalarGridSpec(
            num_scalar_prefetch=AXES,
            grid=(count,),
            in_specs=[
                pl.BlockSpec(
                    (1, two, block_size, part), lambda i, *t, axis=axis: (t[axis][i], 0, 0, step * AXES + axis)
                )
                for axis in range(AXES)
            ],
            out_specs=[pl.BlockSpec((1, block_size, part), lambda i, *t: (i, 0, 0))] * (2 * AXES),
        ),
        out_shape=[jax.ShapeDtypeStruct((count, block_size, part), stored.dtype)] * (2 * AXES),
        cost_estimate=pl.CostEstimate(
            flops=0, transcendentals=0, bytes_accessed=count * two * block_size * part * 4 * AXES
        ),
        name="pick",
    )(*tables, *[stored] * AXES)


def scores_of(query, keys, present):
    scores = lax.dot_general(
        query, keys, (((1,), (1,)), ((), ())), preferred_element_type=jnp.float32
    ) * HEAD_DIM ** (-0.5)
    return jnp.where(present, scores, ABSENT)


def head_columns(head):
    return slice(head * HEAD_DIM, (head + 1) * HEAD_DIM)


def span_units(index_refs, query_refs, here_ref, far_refs, spans, span, first, together):
    per_step = query_refs[0].shape[0] // span
    part = query_refs[0].shape[1]
    units = []
    for local in (first + number for number in range(together)):
        in_group = pl.program_id(1) * per_step + local
        entry = pl.program_id(0) * spans + in_group
        rows = pl.ds(pl.multiple_of(local * span, span), span)
        for axis in range(AXES):
            here_at, far_at = index_refs[axis * 2][entry], index_refs[axis * 2 + 1][entry]
            here_block, far_block = jnp.maximum(here_at, 0), jnp.maximum(far_at, 0)
            for head in range(part // HEAD_DIM):
                columns = head_columns(head)
                here_columns = head_columns(axis * (part // HEAD_DIM) + head)
                query = query_refs[axis][rows, columns]
                here = scores_of(query, here_ref[here_block, 0, :, here_columns], here_at >= 0)
                far = scores_of(query, far_refs[axis][far_block, :, columns], far_at >= 0)
                lane = (in_group * (part // HEAD_DIM) + head) * 2
                units.append((axis, rows, columns, here_block, here_columns, far_block, lane, here, far))
    return units


def stats_kernel(spans, span, together, *refs):
    index_refs, refs = refs[:2 * AXES], refs[2 * AXES:]
    query_refs, here_ref, far_refs, out_refs = refs[:AXES], refs[AXES], refs[AXES + 1:2 * AXES + 1], refs[2 * AXES + 1:]
    turns = query_refs[0].shape[0] // span // together

    @pl.when(pl.program_id(1) == 0)
    def _():
        for out_ref in out_refs:
            out_ref[...] = jnp.zeros_like(out_ref)

    lanes = lax.broadcasted_iota(jnp.int32, out_refs[0].shape[1:], 1)

    def some(turn, carry):
        units = span_units(index_refs, query_refs, here_ref, far_refs, spans, span, turn * together, together)
        tops = [jnp.max(jnp.maximum(unit[-2], unit[-1]), axis=-1, keepdims=True) for unit in units]
        totals = [
            jnp.sum(jnp.exp(unit[-2] - top) + jnp.exp(unit[-1] - top), axis=-1, keepdims=True)
            for unit, top in zip(units, tops)
        ]
        for axis in range(AXES):
            kept = out_refs[axis][0]
            for unit, top, total in zip(units, tops, totals):
                if unit[0] == axis:
                    kept = jnp.where(lanes == unit[6], top, kept)
                    kept = jnp.where(lanes == unit[6] + 1, total, kept)
            out_refs[axis][0] = kept
        return carry

    lax.fori_loop(0, turns, some, 0)


def mix_kernel(spans, span, together, *refs):
    index_refs, refs = refs[:2 * AXES], refs[2 * AXES:]
    query_refs, here_ref, refs = refs[:AXES], refs[AXES], refs[AXES + 1:]
    far_refs, value_refs, mine_refs, their_refs, keep_refs, send_refs = (
        refs[i * AXES:(i + 1) * AXES] for i in range(6)
    )
    turns = query_refs[0].shape[0] // span // together
    lanes = lax.broadcasted_iota(jnp.int32, mine_refs[0].shape[1:], 1)

    def column(stats, at):
        return jnp.sum(jnp.where(lanes == at, stats, 0.0), axis=-1, keepdims=True)

    def some(out_refs, turn, carry):
        units = span_units(index_refs, query_refs, here_ref, far_refs, spans, span, turn * together, together)
        scales = []
        for unit in units:
            mine, theirs, at = mine_refs[unit[0]][0], their_refs[unit[0]][0], unit[6]
            my_top, their_top = column(mine, at), column(theirs, at)
            top = jnp.maximum(my_top, their_top)
            total = column(mine, at + 1) * jnp.exp(my_top - top) + column(theirs, at + 1) * jnp.exp(their_top - top)
            scales.append((top, 1.0 / total))
        weights = [
            jnp.concatenate(
                [jnp.exp(unit[-2] - top) * scale, jnp.exp(unit[-1] - top) * scale], axis=1
            ).astype(jnp.bfloat16)
            for unit, (top, scale) in zip(units, scales)
        ]
        for (axis, rows, columns, here_block, here_columns, far_block, _, _, _), weight in zip(units, weights):
            values = jnp.concatenate(
                [here_ref[here_block, 1, :, here_columns], value_refs[axis][far_block, :, columns]], axis=0
            )
            out_refs[axis][rows, columns] = jnp.dot(weight, values, preferred_element_type=jnp.float32)
        return carry

    for group, out_refs in enumerate((keep_refs, send_refs)):
        @pl.when(pl.program_id(0) == group)
        def _(out_refs=out_refs):
            lax.fori_loop(0, turns, functools.partial(some, out_refs), 0)


def span_call(kernel, indices, queries, stored, received, stats, step, part, spans, planes):
    rows = queries[0].shape[0] // 2
    span = rows // spans
    count, _, block_size, _ = stored.shape
    slots = received[0].shape[0]
    per_step = 8 if spans % 8 == 0 else spans
    steps = spans // per_step
    together = 2 if per_step % 2 == 0 else 1
    step_rows = per_step * span

    in_specs = [pl.BlockSpec((step_rows, part), lambda c, i, *t: (c * steps + i, 0))] * AXES
    in_specs += [pl.BlockSpec((count, planes, block_size, AXES * part), lambda c, i, *t: (0, 0, 0, step))]
    in_specs += [pl.BlockSpec((slots, block_size, part), lambda c, i, *t: (0, 0, 0))] * (planes * AXES)
    if stats:
        in_specs += [pl.BlockSpec((1, span, LANES), lambda c, i, *t: (c, 0, 0))] * AXES
        in_specs += [pl.BlockSpec((1, span, LANES), lambda c, i, *t: (1 - c, 0, 0))] * AXES
        out_specs = [pl.BlockSpec((step_rows, part), lambda c, i, *t: (jnp.where(c == 0, i, steps - 1), 0))] * AXES
        out_specs += [pl.BlockSpec((step_rows, part), lambda c, i, *t: (jnp.where(c == 0, 0, i), 0))] * AXES
        out_shape = [jax.ShapeDtypeStruct((rows, part), jnp.float32)] * (2 * AXES)
    else:
        out_specs = [pl.BlockSpec((1, span, LANES), lambda c, i, *t: (c, 0, 0))] * AXES
        out_shape = [jax.ShapeDtypeStruct((2, span, LANES), jnp.float32)] * AXES
    return pl.pallas_call(
        functools.partial(kernel, spans, span, together),
        grid_spec=pltpu.PrefetchScalarGridSpec(
            num_scalar_prefetch=2 * AXES,
            grid=(2, steps),
            in_specs=in_specs,
            out_specs=out_specs,
        ),
        out_shape=out_shape,
        cost_estimate=pl.CostEstimate(
            flops=8 * rows * NEIGH * block_size * part * AXES * planes,
            transcendentals=2 * rows * NEIGH * block_size * part * AXES // HEAD_DIM,
            bytes_accessed=(count + slots) * planes * block_size * part * 2 * AXES,
        ),
        name="mix" if stats else "stats",
    )(*indices, *queries, stored, *received, *stats)


def exchange_tables(neighbor_shard, neighbor_block, capacity):
    me = lax.axis_index("dp")
    both = jnp.concatenate([neighbor_shard, neighbor_block], axis=1)
    groups = jnp.stack([both] + [over_dp(both, bit) for bit in (1, 2, 3)])
    spans = both.shape[0]
    owners = groups[:, :, :NEIGH].reshape(4, spans * NEIGH)
    wanted = groups[:, :, NEIGH:].reshape(4, spans * NEIGH)
    order = jnp.arange(spans * NEIGH, dtype=jnp.int32)
    same = (owners[:, :, None] == owners[:, None, :]) & (order[None, None, :] < order[None, :, None])
    rank = jnp.sum(same.astype(jnp.int32), axis=2)
    slots = jnp.arange(capacity, dtype=jnp.int32)
    hit = (owners == me)[:, :, None] & (rank[:, :, None] == slots[None, None, :])
    table = jnp.sum(jnp.where(hit, wanted[:, :, None], 0), axis=1)
    sends, places = [], []
    for axis in range(AXES):
        near = 1 << axis
        partner = 3 ^ near
        sends.append(jnp.concatenate([table[near], table[3]]))
        here, far = [], []
        for position, group in enumerate((0, partner)):
            mine = (owners[group] == me).reshape(spans, NEIGH)
            other = (owners[group] == me ^ near).reshape(spans, NEIGH)
            block = wanted[group].reshape(spans, NEIGH)
            slot = rank[group].reshape(spans, NEIGH) + position * capacity
            here.append(jnp.max(jnp.where(mine, block, -1), axis=1))
            far.append(jnp.max(jnp.where(other, slot, -1), axis=1))
        places += [jnp.concatenate(here), jnp.concatenate(far)]
    return sends, places


def after(values, marker):
    return lax.optimization_barrier((values, marker))[0]


def work(tokens, w_query, w_output, neighbor_shard, neighbor_block, kv_store):
    local_width = w_query.shape[1]
    row_count, width = tokens.shape
    peers = lax.axis_size("dp")
    members = lax.axis_size("fsdp")
    passes = 2 if local_width % (2 * AXES * HEAD_DIM) == 0 else 1
    part = local_width // (passes * AXES)
    share = AXES * part
    span_count = neighbor_shard.shape[0]
    capacity = max(2, 3 * span_count * NEIGH // (2 * peers))

    sends, places = exchange_tables(neighbor_shard, neighbor_block, capacity)
    stored = kv_store[0]
    picked = []
    for step in range(passes):
        picked.append(pick_blocks(stored, sends, step, part))

    def query_columns(step):
        columns = w_query[:, step * share:(step + 1) * share]
        if step > 0:
            columns = after(columns, picked[0])
        return lax.all_gather(columns, "dp", axis=0, tiled=True)

    def send_blocks(step, plane, marker):
        blocks = [picked[step][axis * 2 + plane] for axis in range(AXES)]
        if marker is not None:
            blocks = after(blocks, marker)
        return [over_dp(blocks[axis], 1 << axis) for axis in range(AXES)]

    pieces = pieces_over_fsdp(tokens)
    gathered = jnp.zeros((row_count, members * width), tokens.dtype)
    for owner, piece in pieces:
        gathered = lax.dynamic_update_slice(gathered, piece, (0, owner * width))
    normed = normalize(gathered)

    columns = [query_columns(step) for step in range(passes)]
    received = [[send_blocks(0, plane, None) for plane in range(2)]]
    asked, own_queries = [], []
    for step in range(passes):
        queries = jnp.dot(normed, columns[step], preferred_element_type=jnp.float32).astype(jnp.bfloat16)
        own_queries.append(queries)
        parts = [queries[:, axis * part:(axis + 1) * part] for axis in range(AXES)]
        asked.append([
            jnp.concatenate([parts[axis], over_dp(parts[axis], 3 ^ (1 << axis))], axis=0) for axis in range(AXES)
        ])
        if step > 0:
            received.append([send_blocks(step, 0, own_queries[0]), send_blocks(step, 1, queries)])
    w_output = after(w_output, own_queries[-1])
    w_output_columns = lax.all_gather(w_output, "dp", axis=0, tiled=True)

    attended = jnp.zeros((row_count, members * local_width), jnp.bfloat16)
    for step in range(passes):
        common = dict(step=step, part=part, spans=span_count)
        mine = span_call(
            stats_kernel, places, asked[step], stored, received[step][0], [], planes=1, **common
        )
        theirs = [over_dp(mine[axis], 3 ^ (1 << axis)) for axis in range(AXES)]
        partial = span_call(
            mix_kernel, places, asked[step], stored, received[step][0] + received[step][1], list(mine) + theirs,
            planes=2, **common
        )
        others = [over_dp(partial[AXES + axis], 3 ^ (1 << axis)) for axis in range(AXES)]
        mixed = jnp.concatenate(
            [(partial[axis] + others[axis]).astype(jnp.bfloat16) for axis in range(AXES)], axis=1
        )
        pieces = pieces_over_fsdp(mixed)
        for owner, piece in pieces:
            start = owner * local_width + step * share
            attended = lax.dynamic_update_slice(attended, piece, (0, start))
    summed = jnp.dot(attended, w_output_columns, preferred_element_type=jnp.float32)
    return summed.astype(jnp.bfloat16)


def solution(mesh):
    in_specs = (
        P("dp", "fsdp"),
        P("dp", "fsdp"),
        P("dp", "fsdp"),
        P("dp", None),
        P("dp", None),
        P("dp", None, None, None, "fsdp"),
    )
    out_specs = P("dp", "fsdp")
    return jax.shard_map(work, mesh=mesh, in_specs=in_specs, out_specs=out_specs, check_vma=False)
```

```python
import functools

import jax
import jax.numpy as jnp
from jax import lax
from jax.experimental import pallas as pl
from jax.experimental.pallas import tpu as pltpu
from jax.sharding import PartitionSpec as P


HEAD_DIM = 128
NEIGH = 2
AXES = 2
LANES = 128
ABSENT = -1e30

EPSILON = 1e-05


def normalize(features):
    widened = features.astype(jnp.float32)
    mean_square = jnp.mean(widened * widened, axis=1, keepdims=True)
    return (widened * lax.rsqrt(mean_square + EPSILON)).astype(jnp.bfloat16)


def over_dp(value, bit):
    return lax.ppermute(value, "dp", [(i, i ^ bit) for i in range(lax.axis_size("dp"))])


def pieces_over_fsdp(piece):
    members = lax.axis_size("fsdp")
    chips = members // 2
    if chips != 4:
        whole = lax.all_gather(piece, "fsdp", axis=0)
        return [(i, whole[i]) for i in range(members)]
    me = lax.axis_index("fsdp")
    chip, core = me // 2, me % 2

    def chip_pairs(pairs):
        return [(a * 2 + c, b * 2 + c) for a, b in pairs for c in range(2)]

    def swap(value):
        return lax.ppermute(value, "fsdp", [(i, i ^ 1) for i in range(members)])

    back2 = lax.ppermute(piece, "fsdp", chip_pairs([(0, 2), (1, 3), (2, 0), (3, 1)]))
    back1 = lax.ppermute(piece, "fsdp", chip_pairs([(0, 1), (1, 2), (2, 3)]))
    back3 = lax.ppermute(piece, "fsdp", chip_pairs([(1, 0), (2, 1), (3, 2)]))
    own_there = swap(piece)
    ends = lax.ppermute(back2, "fsdp", chip_pairs([(2, 3), (1, 0)]))
    there1, there2, there3 = swap(back1), swap(back2), swap(back3)
    ends_there = lax.ppermute(ends, "fsdp", [(0, 1), (1, 0), (6, 7), (7, 6)])
    found = []
    for step, (here, there) in enumerate((
        (piece, own_there),
        (jnp.where(chip == 0, ends, back1), jnp.where(chip == 0, ends_there, there1)),
        (back2, there2),
        (jnp.where(chip == 3, ends, back3), jnp.where(chip == 3, ends_there, there3)),
    )):
        owner = (chip + 4 - step) % 4
        found.append((owner * 2 + core, here))
        found.append((owner * 2 + 1 - core, there))
    return found


def pick_kernel(first_ref, second_ref, *refs):
    for axis in range(AXES):
        for plane in range(2):
            refs[AXES + axis * 2 + plane][...] = refs[axis][:, plane]


def pick_blocks(stored, tables, step, part):
    count = tables[0].shape[0]
    _, two, block_size, _ = stored.shape
    return pl.pallas_call(
        pick_kernel,
        grid_spec=pltpu.PrefetchScalarGridSpec(
            num_scalar_prefetch=AXES,
            grid=(count,),
            in_specs=[
                pl.BlockSpec(
                    (1, two, block_size, part), lambda i, *t, axis=axis: (t[axis][i], 0, 0, step * AXES + axis)
                )
                for axis in range(AXES)
            ],
            out_specs=[pl.BlockSpec((1, block_size, part), lambda i, *t: (i, 0, 0))] * (2 * AXES),
        ),
        out_shape=[jax.ShapeDtypeStruct((count, block_size, part), stored.dtype)] * (2 * AXES),
        cost_estimate=pl.CostEstimate(
            flops=0, transcendentals=0, bytes_accessed=count * two * block_size * part * 4 * AXES
        ),
        name="pick",
    )(*tables, *[stored] * AXES)


def scores_of(query, keys, present):
    scores = lax.dot_general(
        query, keys, (((1,), (1,)), ((), ())), preferred_element_type=jnp.float32
    ) * HEAD_DIM ** (-0.5)
    return jnp.where(present, scores, ABSENT)


def head_columns(head):
    return slice(head * HEAD_DIM, (head + 1) * HEAD_DIM)


def span_units(index_refs, query_refs, here_ref, far_refs, spans, span, first, together):
    per_step = query_refs[0].shape[0] // span
    part = query_refs[0].shape[1]
    units = []
    for local in (first + number for number in range(together)):
        in_group = pl.program_id(1) * per_step + local
        entry = pl.program_id(0) * spans + in_group
        rows = pl.ds(pl.multiple_of(local * span, span), span)
        for axis in range(AXES):
            here_at, far_at = index_refs[axis * 2][entry], index_refs[axis * 2 + 1][entry]
            here_block, far_block = jnp.maximum(here_at, 0), jnp.maximum(far_at, 0)
            for head in range(part // HEAD_DIM):
                columns = head_columns(head)
                here_columns = head_columns(axis * (part // HEAD_DIM) + head)
                query = query_refs[axis][rows, columns]
                here = scores_of(query, here_ref[here_block, 0, :, here_columns], here_at >= 0)
                far = scores_of(query, far_refs[axis][far_block, :, columns], far_at >= 0)
                lane = (in_group * (part // HEAD_DIM) + head) * 2
                units.append((axis, rows, columns, here_block, here_columns, far_block, lane, here, far))
    return units


def stats_kernel(spans, span, together, *refs):
    index_refs, refs = refs[:2 * AXES], refs[2 * AXES:]
    query_refs, here_ref, far_refs, out_refs = refs[:AXES], refs[AXES], refs[AXES + 1:2 * AXES + 1], refs[2 * AXES + 1:]
    turns = query_refs[0].shape[0] // span // together

    @pl.when(pl.program_id(1) == 0)
    def _():
        for out_ref in out_refs:
            out_ref[...] = jnp.zeros_like(out_ref)

    lanes = lax.broadcasted_iota(jnp.int32, out_refs[0].shape[1:], 1)

    def some(turn, carry):
        units = span_units(index_refs, query_refs, here_ref, far_refs, spans, span, turn * together, together)
        tops = [jnp.max(jnp.maximum(unit[-2], unit[-1]), axis=-1, keepdims=True) for unit in units]
        totals = [
            jnp.sum(jnp.exp(unit[-2] - top) + jnp.exp(unit[-1] - top), axis=-1, keepdims=True)
            for unit, top in zip(units, tops)
        ]
        for axis in range(AXES):
            kept = out_refs[axis][0]
            for unit, top, total in zip(units, tops, totals):
                if unit[0] == axis:
                    kept = jnp.where(lanes == unit[6], top, kept)
                    kept = jnp.where(lanes == unit[6] + 1, total, kept)
            out_refs[axis][0] = kept
        return carry

    lax.fori_loop(0, turns, some, 0)


def mix_kernel(spans, span, together, *refs):
    index_refs, refs = refs[:2 * AXES], refs[2 * AXES:]
    query_refs, here_ref, refs = refs[:AXES], refs[AXES], refs[AXES + 1:]
    far_refs, value_refs, mine_refs, their_refs, keep_refs, send_refs = (
        refs[i * AXES:(i + 1) * AXES] for i in range(6)
    )
    turns = query_refs[0].shape[0] // span // together
    lanes = lax.broadcasted_iota(jnp.int32, mine_refs[0].shape[1:], 1)

    def column(stats, at):
        return jnp.sum(jnp.where(lanes == at, stats, 0.0), axis=-1, keepdims=True)

    def some(out_refs, turn, carry):
        units = span_units(index_refs, query_refs, here_ref, far_refs, spans, span, turn * together, together)
        scales = []
        for unit in units:
            mine, theirs, at = mine_refs[unit[0]][0], their_refs[unit[0]][0], unit[6]
            my_top, their_top = column(mine, at), column(theirs, at)
            top = jnp.maximum(my_top, their_top)
            total = column(mine, at + 1) * jnp.exp(my_top - top) + column(theirs, at + 1) * jnp.exp(their_top - top)
            scales.append((top, 1.0 / total))
        weights = [
            jnp.concatenate(
                [jnp.exp(unit[-2] - top) * scale, jnp.exp(unit[-1] - top) * scale], axis=1
            ).astype(jnp.bfloat16)
            for unit, (top, scale) in zip(units, scales)
        ]
        for (axis, rows, columns, here_block, here_columns, far_block, _, _, _), weight in zip(units, weights):
            values = jnp.concatenate(
                [here_ref[here_block, 1, :, here_columns], value_refs[axis][far_block, :, columns]], axis=0
            )
            out_refs[axis][rows, columns] = jnp.dot(weight, values, preferred_element_type=jnp.float32)
        return carry

    for group, out_refs in enumerate((keep_refs, send_refs)):
        @pl.when(pl.program_id(0) == group)
        def _(out_refs=out_refs):
            lax.fori_loop(0, turns, functools.partial(some, out_refs), 0)


def span_call(kernel, indices, queries, stored, received, stats, step, part, spans, planes):
    rows = queries[0].shape[0] // 2
    span = rows // spans
    count, _, block_size, _ = stored.shape
    slots = received[0].shape[0]
    per_step = 8 if spans % 8 == 0 else spans
    steps = spans // per_step
    together = 2 if per_step % 2 == 0 and not stats else 1
    step_rows = per_step * span

    in_specs = [pl.BlockSpec((step_rows, part), lambda c, i, *t: (c * steps + i, 0))] * AXES
    in_specs += [pl.BlockSpec((count, planes, block_size, AXES * part), lambda c, i, *t: (0, 0, 0, step))]
    in_specs += [pl.BlockSpec((slots, block_size, part), lambda c, i, *t: (0, 0, 0))] * (planes * AXES)
    if stats:
        in_specs += [pl.BlockSpec((1, span, LANES), lambda c, i, *t: (c, 0, 0))] * AXES
        in_specs += [pl.BlockSpec((1, span, LANES), lambda c, i, *t: (1 - c, 0, 0))] * AXES
        out_specs = [pl.BlockSpec((step_rows, part), lambda c, i, *t: (jnp.where(c == 0, i, steps - 1), 0))] * AXES
        out_specs += [pl.BlockSpec((step_rows, part), lambda c, i, *t: (jnp.where(c == 0, 0, i), 0))] * AXES
        out_shape = [jax.ShapeDtypeStruct((rows, part), jnp.float32)] * (2 * AXES)
    else:
        out_specs = [pl.BlockSpec((1, span, LANES), lambda c, i, *t: (c, 0, 0))] * AXES
        out_shape = [jax.ShapeDtypeStruct((2, span, LANES), jnp.float32)] * AXES
    return pl.pallas_call(
        functools.partial(kernel, spans, span, together),
        grid_spec=pltpu.PrefetchScalarGridSpec(
            num_scalar_prefetch=2 * AXES,
            grid=(2, steps),
            in_specs=in_specs,
            out_specs=out_specs,
        ),
        out_shape=out_shape,
        cost_estimate=pl.CostEstimate(
            flops=8 * rows * NEIGH * block_size * part * AXES * planes,
            transcendentals=2 * rows * NEIGH * block_size * part * AXES // HEAD_DIM,
            bytes_accessed=(count + slots) * planes * block_size * part * 2 * AXES,
        ),
        name="mix" if stats else "stats",
    )(*indices, *queries, stored, *received, *stats)


def exchange_tables(neighbor_shard, neighbor_block, capacity):
    me = lax.axis_index("dp")
    both = jnp.concatenate([neighbor_shard, neighbor_block], axis=1)
    groups = jnp.stack([both] + [over_dp(both, bit) for bit in (1, 2, 3)])
    spans = both.shape[0]
    owners = groups[:, :, :NEIGH].reshape(4, spans * NEIGH)
    wanted = groups[:, :, NEIGH:].reshape(4, spans * NEIGH)
    order = jnp.arange(spans * NEIGH, dtype=jnp.int32)
    same = (owners[:, :, None] == owners[:, None, :]) & (order[None, None, :] < order[None, :, None])
    rank = jnp.sum(same.astype(jnp.int32), axis=2)
    slots = jnp.arange(capacity, dtype=jnp.int32)
    hit = (owners == me)[:, :, None] & (rank[:, :, None] == slots[None, None, :])
    table = jnp.sum(jnp.where(hit, wanted[:, :, None], 0), axis=1)
    sends, places = [], []
    for axis in range(AXES):
        near = 1 << axis
        partner = 3 ^ near
        sends.append(jnp.concatenate([table[near], table[3]]))
        here, far = [], []
        for position, group in enumerate((0, partner)):
            mine = (owners[group] == me).reshape(spans, NEIGH)
            other = (owners[group] == me ^ near).reshape(spans, NEIGH)
            block = wanted[group].reshape(spans, NEIGH)
            slot = rank[group].reshape(spans, NEIGH) + position * capacity
            here.append(jnp.max(jnp.where(mine, block, -1), axis=1))
            far.append(jnp.max(jnp.where(other, slot, -1), axis=1))
        places += [jnp.concatenate(here), jnp.concatenate(far)]
    return sends, places


def after(values, marker):
    return lax.optimization_barrier((values, marker))[0]


def work(tokens, w_query, w_output, neighbor_shard, neighbor_block, kv_store):
    local_width = w_query.shape[1]
    row_count, width = tokens.shape
    peers = lax.axis_size("dp")
    members = lax.axis_size("fsdp")
    passes = 2 if local_width % (2 * AXES * HEAD_DIM) == 0 else 1
    part = local_width // (passes * AXES)
    share = local_width // passes
    span_count = neighbor_shard.shape[0]
    capacity = max(2, 3 * span_count * NEIGH // (2 * peers))

    sends, places = exchange_tables(neighbor_shard, neighbor_block, capacity)
    stored = kv_store[0]
    picked = []
    for step in range(passes):
        picked.append(pick_blocks(stored, sends, step, part))

    def query_columns(step):
        columns = w_query[:, step * share:(step + 1) * share]
        if step > 0:
            columns = after(columns, picked[0])
        return lax.all_gather(columns, "dp", axis=0, tiled=True)

    def send_blocks(step, plane, marker):
        blocks = [picked[step][axis * 2 + plane] for axis in range(AXES)]
        if marker is not None:
            blocks = after(blocks, marker)
        return [over_dp(blocks[axis], 1 << axis) for axis in range(AXES)]

    pieces = pieces_over_fsdp(tokens)
    gathered = jnp.zeros((row_count, members * width), tokens.dtype)
    for owner, piece in pieces:
        gathered = lax.dynamic_update_slice(gathered, piece, (0, owner * width))
    normed = normalize(gathered)

    columns = [query_columns(step) for step in range(passes)]
    received = [[send_blocks(0, plane, None) for plane in range(2)]]
    asked, own_queries = [], []
    for step in range(passes):
        queries = jnp.dot(normed, columns[step], preferred_element_type=jnp.float32).astype(jnp.bfloat16)
        own_queries.append(queries)
        parts = [queries[:, axis * part:(axis + 1) * part] for axis in range(AXES)]
        asked.append([
            jnp.concatenate([parts[axis], over_dp(parts[axis], 3 ^ (1 << axis))], axis=0) for axis in range(AXES)
        ])
        if step > 0:
            received.append([send_blocks(step, 0, own_queries[0]), send_blocks(step, 1, queries)])

    attended = gathered
    if width != local_width:
        attended = jnp.zeros((row_count, members * local_width), jnp.bfloat16)
    for step in range(passes):
        common = dict(step=step, part=part, spans=span_count)
        mine = span_call(
            stats_kernel, places, asked[step], stored, received[step][0], [], planes=1, **common
        )
        if step == passes - 1:
            output_columns = lax.all_gather(after(w_output, mine), "dp", axis=0, tiled=True)
        theirs = [over_dp(mine[axis], 3 ^ (1 << axis)) for axis in range(AXES)]
        partial = span_call(
            mix_kernel, places, asked[step], stored, received[step][0] + received[step][1], list(mine) + theirs,
            planes=2, **common
        )
        others = [over_dp(partial[AXES + axis], 3 ^ (1 << axis)) for axis in range(AXES)]
        mixed = jnp.concatenate(
            [(partial[axis] + others[axis]).astype(jnp.bfloat16) for axis in range(AXES)], axis=1
        )
        pieces = pieces_over_fsdp(mixed)
        for owner, piece in pieces:
            start = owner * local_width + step * share
            attended = lax.dynamic_update_slice(attended, piece, (0, start))
    summed = jnp.dot(attended, output_columns, preferred_element_type=jnp.float32)
    return summed.astype(jnp.bfloat16)


def solution(mesh):
    in_specs = (
        P("dp", "fsdp"),
        P("dp", "fsdp"),
        P("dp", "fsdp"),
        P("dp", None),
        P("dp", None),
        P("dp", None, None, None, "fsdp"),
    )
    out_specs = P("dp", "fsdp")
    return jax.shard_map(work, mesh=mesh, in_specs=in_specs, out_specs=out_specs, check_vma=False)
```

```python
import functools

import jax
import jax.numpy as jnp
from jax import lax
from jax.experimental import pallas as pl
from jax.experimental.pallas import tpu as pltpu
from jax.sharding import PartitionSpec as P


HEAD_DIM = 128
NEIGH = 2
AXES = 2
LANES = 128
ABSENT = -1e30

EPSILON = 1e-05


def normalize(features):
    widened = features.astype(jnp.float32)
    mean_square = jnp.mean(widened * widened, axis=1, keepdims=True)
    return (widened * lax.rsqrt(mean_square + EPSILON)).astype(jnp.bfloat16)


def over_dp(value, bit):
    return lax.ppermute(value, "dp", [(i, i ^ bit) for i in range(lax.axis_size("dp"))])


def pieces_over_fsdp(piece):
    members = lax.axis_size("fsdp")
    chips = members // 2
    if chips != 4:
        whole = lax.all_gather(piece, "fsdp", axis=0)
        return [(i, whole[i]) for i in range(members)]
    me = lax.axis_index("fsdp")
    chip, core = me // 2, me % 2

    def chip_pairs(pairs):
        return [(a * 2 + c, b * 2 + c) for a, b in pairs for c in range(2)]

    def swap(value):
        return lax.ppermute(value, "fsdp", [(i, i ^ 1) for i in range(members)])

    back2 = lax.ppermute(piece, "fsdp", chip_pairs([(0, 2), (1, 3), (2, 0), (3, 1)]))
    back1 = lax.ppermute(piece, "fsdp", chip_pairs([(0, 1), (1, 2), (2, 3)]))
    back3 = lax.ppermute(piece, "fsdp", chip_pairs([(1, 0), (2, 1), (3, 2)]))
    own_there = swap(piece)
    ends = lax.ppermute(back2, "fsdp", chip_pairs([(2, 3), (1, 0)]))
    there2 = swap(back2)
    there1, there3 = swap(back1), swap(back3)
    ends_there = lax.ppermute(ends, "fsdp", [(0, 1), (1, 0), (6, 7), (7, 6)])
    found = []
    for step, (here, there) in enumerate((
        (piece, own_there),
        (back2, there2),
        (jnp.where(chip == 0, ends, back1), jnp.where(chip == 0, ends_there, there1)),
        (jnp.where(chip == 3, ends, back3), jnp.where(chip == 3, ends_there, there3)),
    )):
        owner = (chip + 4 - (0, 2, 1, 3)[step]) % 4
        found.append((owner * 2 + core, here))
        found.append((owner * 2 + 1 - core, there))
    return found


def pick_kernel(first_ref, second_ref, *refs):
    for axis in range(AXES):
        for plane in range(2):
            refs[AXES + axis * 2 + plane][...] = refs[axis][:, plane]


def pick_blocks(stored, tables, step, part):
    count = tables[0].shape[0]
    _, two, block_size, _ = stored.shape
    return pl.pallas_call(
        pick_kernel,
        grid_spec=pltpu.PrefetchScalarGridSpec(
            num_scalar_prefetch=AXES,
            grid=(count,),
            in_specs=[
                pl.BlockSpec(
                    (1, two, block_size, part), lambda i, *t, axis=axis: (t[axis][i], 0, 0, step * AXES + axis)
                )
                for axis in range(AXES)
            ],
            out_specs=[pl.BlockSpec((1, block_size, part), lambda i, *t: (i, 0, 0))] * (2 * AXES),
        ),
        out_shape=[jax.ShapeDtypeStruct((count, block_size, part), stored.dtype)] * (2 * AXES),
        cost_estimate=pl.CostEstimate(
            flops=0, transcendentals=0, bytes_accessed=count * two * block_size * part * 4 * AXES
        ),
        name="pick",
    )(*tables, *[stored] * AXES)


def scores_of(query, keys, present):
    scores = lax.dot_general(
        query, keys, (((1,), (1,)), ((), ())), preferred_element_type=jnp.float32
    ) * HEAD_DIM ** (-0.5)
    return jnp.where(present, scores, ABSENT)


def head_columns(head):
    return slice(head * HEAD_DIM, (head + 1) * HEAD_DIM)


def span_units(index_refs, query_refs, here_ref, far_refs, spans, span, first, together):
    per_step = query_refs[0].shape[0] // span
    part = query_refs[0].shape[1]
    units = []
    for local in (first + number for number in range(together)):
        in_group = pl.program_id(1) * per_step + local
        entry = pl.program_id(0) * spans + in_group
        rows = pl.ds(pl.multiple_of(local * span, span), span)
        for axis in range(AXES):
            here_at, far_at = index_refs[axis * 2][entry], index_refs[axis * 2 + 1][entry]
            here_block, far_block = jnp.maximum(here_at, 0), jnp.maximum(far_at, 0)
            for head in range(part // HEAD_DIM):
                columns = head_columns(head)
                here_columns = head_columns(axis * (part // HEAD_DIM) + head)
                query = query_refs[axis][rows, columns]
                here = scores_of(query, here_ref[here_block, 0, :, here_columns], here_at >= 0)
                far = scores_of(query, far_refs[axis][far_block, :, columns], far_at >= 0)
                lane = (in_group * (part // HEAD_DIM) + head) * 2
                units.append((axis, rows, columns, here_block, here_columns, far_block, lane, here, far))
    return units


def stats_kernel(spans, span, together, *refs):
    index_refs, refs = refs[:2 * AXES], refs[2 * AXES:]
    query_refs, here_ref, far_refs, out_refs = refs[:AXES], refs[AXES], refs[AXES + 1:2 * AXES + 1], refs[2 * AXES + 1:]
    turns = query_refs[0].shape[0] // span // together

    @pl.when(pl.program_id(1) == 0)
    def _():
        for out_ref in out_refs:
            out_ref[...] = jnp.zeros_like(out_ref)

    lanes = lax.broadcasted_iota(jnp.int32, out_refs[0].shape[1:], 1)

    def some(turn, carry):
        units = span_units(index_refs, query_refs, here_ref, far_refs, spans, span, turn * together, together)
        tops = [jnp.max(jnp.maximum(unit[-2], unit[-1]), axis=-1, keepdims=True) for unit in units]
        totals = [
            jnp.sum(jnp.exp(unit[-2] - top) + jnp.exp(unit[-1] - top), axis=-1, keepdims=True)
            for unit, top in zip(units, tops)
        ]
        for axis in range(AXES):
            kept = out_refs[axis][0]
            for unit, top, total in zip(units, tops, totals):
                if unit[0] == axis:
                    kept = jnp.where(lanes == unit[6], top, kept)
                    kept = jnp.where(lanes == unit[6] + 1, total, kept)
            out_refs[axis][0] = kept
        return carry

    lax.fori_loop(0, turns, some, 0)


def mix_kernel(spans, span, together, *refs):
    index_refs, refs = refs[:2 * AXES], refs[2 * AXES:]
    query_refs, here_ref, refs = refs[:AXES], refs[AXES], refs[AXES + 1:]
    far_refs, value_refs, mine_refs, their_refs, keep_refs, send_refs = (
        refs[i * AXES:(i + 1) * AXES] for i in range(6)
    )
    turns = query_refs[0].shape[0] // span // together
    lanes = lax.broadcasted_iota(jnp.int32, mine_refs[0].shape[1:], 1)

    def column(stats, at):
        return jnp.sum(jnp.where(lanes == at, stats, 0.0), axis=-1, keepdims=True)

    def some(out_refs, turn, carry):
        units = span_units(index_refs, query_refs, here_ref, far_refs, spans, span, turn * together, together)
        scales = []
        for unit in units:
            mine, theirs, at = mine_refs[unit[0]][0], their_refs[unit[0]][0], unit[6]
            my_top, their_top = column(mine, at), column(theirs, at)
            top = jnp.maximum(my_top, their_top)
            total = column(mine, at + 1) * jnp.exp(my_top - top) + column(theirs, at + 1) * jnp.exp(their_top - top)
            scales.append((top, 1.0 / total))
        weights = [
            jnp.concatenate(
                [jnp.exp(unit[-2] - top) * scale, jnp.exp(unit[-1] - top) * scale], axis=1
            ).astype(jnp.bfloat16)
            for unit, (top, scale) in zip(units, scales)
        ]
        for (axis, rows, columns, here_block, here_columns, far_block, _, _, _), weight in zip(units, weights):
            values = jnp.concatenate(
                [here_ref[here_block, 1, :, here_columns], value_refs[axis][far_block, :, columns]], axis=0
            )
            out_refs[axis][rows, columns] = jnp.dot(weight, values, preferred_element_type=jnp.float32)
        return carry

    for group, out_refs in enumerate((keep_refs, send_refs)):
        @pl.when(pl.program_id(0) == group)
        def _(out_refs=out_refs):
            lax.fori_loop(0, turns, functools.partial(some, out_refs), 0)


def span_call(kernel, indices, queries, stored, received, stats, step, part, spans, planes):
    rows = queries[0].shape[0] // 2
    span = rows // spans
    count, _, block_size, _ = stored.shape
    slots = received[0].shape[0]
    per_step = 8 if spans % 8 == 0 else spans
    steps = spans // per_step
    together = 2 if per_step % 2 == 0 and not stats else 1
    step_rows = per_step * span

    in_specs = [pl.BlockSpec((step_rows, part), lambda c, i, *t: (c * steps + i, 0))] * AXES
    in_specs += [pl.BlockSpec((count, planes, block_size, AXES * part), lambda c, i, *t: (0, 0, 0, step))]
    in_specs += [pl.BlockSpec((slots, block_size, part), lambda c, i, *t: (0, 0, 0))] * (planes * AXES)
    if stats:
        in_specs += [pl.BlockSpec((1, span, LANES), lambda c, i, *t: (c, 0, 0))] * AXES
        in_specs += [pl.BlockSpec((1, span, LANES), lambda c, i, *t: (1 - c, 0, 0))] * AXES
        out_specs = [pl.BlockSpec((step_rows, part), lambda c, i, *t: (jnp.where(c == 0, i, steps - 1), 0))] * AXES
        out_specs += [pl.BlockSpec((step_rows, part), lambda c, i, *t: (jnp.where(c == 0, 0, i), 0))] * AXES
        out_shape = [jax.ShapeDtypeStruct((rows, part), jnp.float32)] * (2 * AXES)
    else:
        out_specs = [pl.BlockSpec((1, span, LANES), lambda c, i, *t: (c, 0, 0))] * AXES
        out_shape = [jax.ShapeDtypeStruct((2, span, LANES), jnp.float32)] * AXES
    return pl.pallas_call(
        functools.partial(kernel, spans, span, together),
        grid_spec=pltpu.PrefetchScalarGridSpec(
            num_scalar_prefetch=2 * AXES,
            grid=(2, steps),
            in_specs=in_specs,
            out_specs=out_specs,
        ),
        out_shape=out_shape,
        cost_estimate=pl.CostEstimate(
            flops=8 * rows * NEIGH * block_size * part * AXES * planes,
            transcendentals=2 * rows * NEIGH * block_size * part * AXES // HEAD_DIM,
            bytes_accessed=(count + slots) * planes * block_size * part * 2 * AXES,
        ),
        name="mix" if stats else "stats",
    )(*indices, *queries, stored, *received, *stats)


def exchange_tables(neighbor_shard, neighbor_block, capacity):
    me = lax.axis_index("dp")
    both = jnp.concatenate([neighbor_shard, neighbor_block], axis=1)
    groups = jnp.stack([both] + [over_dp(both, bit) for bit in (1, 2, 3)])
    spans = both.shape[0]
    owners = groups[:, :, :NEIGH].reshape(4, spans * NEIGH)
    wanted = groups[:, :, NEIGH:].reshape(4, spans * NEIGH)
    order = jnp.arange(spans * NEIGH, dtype=jnp.int32)
    same = (owners[:, :, None] == owners[:, None, :]) & (order[None, None, :] < order[None, :, None])
    rank = jnp.sum(same.astype(jnp.int32), axis=2)
    slots = jnp.arange(capacity, dtype=jnp.int32)
    hit = (owners == me)[:, :, None] & (rank[:, :, None] == slots[None, None, :])
    table = jnp.sum(jnp.where(hit, wanted[:, :, None], 0), axis=1)
    sends, places = [], []
    for axis in range(AXES):
        near = 1 << axis
        partner = 3 ^ near
        sends.append(jnp.concatenate([table[near], table[3]]))
        here, far = [], []
        for position, group in enumerate((0, partner)):
            mine = (owners[group] == me).reshape(spans, NEIGH)
            other = (owners[group] == me ^ near).reshape(spans, NEIGH)
            block = wanted[group].reshape(spans, NEIGH)
            slot = rank[group].reshape(spans, NEIGH) + position * capacity
            here.append(jnp.max(jnp.where(mine, block, -1), axis=1))
            far.append(jnp.max(jnp.where(other, slot, -1), axis=1))
        places += [jnp.concatenate(here), jnp.concatenate(far)]
    return sends, places


def after(values, marker):
    return lax.optimization_barrier((values, marker))[0]


def work(tokens, w_query, w_output, neighbor_shard, neighbor_block, kv_store):
    local_width = w_query.shape[1]
    row_count, width = tokens.shape
    peers = lax.axis_size("dp")
    members = lax.axis_size("fsdp")
    passes = 2 if local_width % (2 * AXES * HEAD_DIM) == 0 else 1
    part = local_width // (passes * AXES)
    share = local_width // passes
    span_count = neighbor_shard.shape[0]
    capacity = max(2, 3 * span_count * NEIGH // (2 * peers))

    sends, places = exchange_tables(neighbor_shard, neighbor_block, capacity)
    stored = kv_store[0]
    picked = []
    for step in range(passes):
        picked.append(pick_blocks(stored, sends, step, part))

    def query_columns(step):
        columns = w_query[:, step * share:(step + 1) * share]
        if step > 0:
            columns = after(columns, picked[0])
        return lax.all_gather(columns, "dp", axis=0, tiled=True)

    def send_blocks(step, plane, marker):
        blocks = [picked[step][axis * 2 + plane] for axis in range(AXES)]
        if marker is not None:
            blocks = after(blocks, marker)
        return [over_dp(blocks[axis], 1 << axis) for axis in range(AXES)]

    pieces = pieces_over_fsdp(tokens)
    gathered = jnp.zeros((row_count, members * width), tokens.dtype)
    for owner, piece in pieces:
        gathered = lax.dynamic_update_slice(gathered, piece, (0, owner * width))
    normed = normalize(gathered)

    columns = [query_columns(step) for step in range(passes)]
    received = [[send_blocks(0, plane, None) for plane in range(2)]]
    asked, own_queries = [], []
    for step in range(passes):
        queries = jnp.dot(normed, columns[step], preferred_element_type=jnp.float32).astype(jnp.bfloat16)
        own_queries.append(queries)
        parts = [queries[:, axis * part:(axis + 1) * part] for axis in range(AXES)]
        asked.append([
            jnp.concatenate([parts[axis], over_dp(parts[axis], 3 ^ (1 << axis))], axis=0) for axis in range(AXES)
        ])
        if step > 0:
            received.append([send_blocks(step, 0, own_queries[0]), send_blocks(step, 1, queries)])

    attended = gathered
    if width != local_width:
        attended = jnp.zeros((row_count, members * local_width), jnp.bfloat16)
    for step in range(passes):
        common = dict(step=step, part=part, spans=span_count)
        mine = span_call(
            stats_kernel, places, asked[step], stored, received[step][0], [], planes=1, **common
        )
        if step == passes - 1:
            output_columns = lax.all_gather(after(w_output, mine), "dp", axis=0, tiled=True)
        theirs = [over_dp(mine[axis], 3 ^ (1 << axis)) for axis in range(AXES)]
        partial = span_call(
            mix_kernel, places, asked[step], stored, received[step][0] + received[step][1], list(mine) + theirs,
            planes=2, **common
        )
        others = [over_dp(partial[AXES + axis], 3 ^ (1 << axis)) for axis in range(AXES)]
        mixed = jnp.concatenate(
            [(partial[axis] + others[axis]).astype(jnp.bfloat16) for axis in range(AXES)], axis=1
        )
        mixed = lax.optimization_barrier(mixed)
        pieces = pieces_over_fsdp(mixed)
        for owner, piece in pieces:
            start = owner * local_width + step * share
            attended = lax.dynamic_update_slice(attended, piece, (0, start))
    summed = jnp.dot(attended, output_columns, preferred_element_type=jnp.float32)
    return summed.astype(jnp.bfloat16)


def solution(mesh):
    in_specs = (
        P("dp", "fsdp"),
        P("dp", "fsdp"),
        P("dp", "fsdp"),
        P("dp", None),
        P("dp", None),
        P("dp", None, None, None, "fsdp"),
    )
    out_specs = P("dp", "fsdp")
    return jax.shard_map(work, mesh=mesh, in_specs=in_specs, out_specs=out_specs, check_vma=False)
```

```python
import functools

import jax
import jax.numpy as jnp
from jax import lax
from jax.experimental import pallas as pl
from jax.experimental.pallas import tpu as pltpu
from jax.sharding import PartitionSpec as P


HEAD_DIM = 128
NEIGH = 2
AXES = 2
LANES = 128
ABSENT = -1e30

EPSILON = 1e-05


def normalize(features):
    widened = features.astype(jnp.float32)
    mean_square = jnp.mean(widened * widened, axis=1, keepdims=True)
    return (widened * lax.rsqrt(mean_square + EPSILON)).astype(jnp.bfloat16)


def over_dp(value, bit):
    return lax.ppermute(value, "dp", [(i, i ^ bit) for i in range(lax.axis_size("dp"))])


def pieces_over_fsdp(piece):
    members = lax.axis_size("fsdp")
    chips = members // 2
    if chips != 4:
        whole = lax.all_gather(piece, "fsdp", axis=0)
        return [(i, whole[i]) for i in range(members)]
    me = lax.axis_index("fsdp")
    chip, core = me // 2, me % 2

    def chip_pairs(pairs):
        return [(a * 2 + c, b * 2 + c) for a, b in pairs for c in range(2)]

    def swap(value):
        return lax.ppermute(value, "fsdp", [(i, i ^ 1) for i in range(members)])

    back2 = lax.ppermute(piece, "fsdp", chip_pairs([(0, 2), (1, 3), (2, 0), (3, 1)]))
    back1 = lax.ppermute(piece, "fsdp", chip_pairs([(0, 1), (1, 2), (2, 3)]))
    back3 = lax.ppermute(piece, "fsdp", chip_pairs([(1, 0), (2, 1), (3, 2)]))
    own_there = swap(piece)
    ends = lax.ppermute(back2, "fsdp", chip_pairs([(2, 3), (1, 0)]))
    there2 = swap(back2)
    there1, there3 = swap(back1), swap(back3)
    ends_there = lax.ppermute(ends, "fsdp", [(0, 1), (1, 0), (6, 7), (7, 6)])
    found = [(chip * 2 + core, piece), (chip * 2 + 1 - core, own_there)]
    for step, value, side in (
        (2, back2, core), (2, there2, 1 - core), (1, back1, core), (3, back3, core), (1, there1, 1 - core), (3, there3, 1 - core)
    ):
        found.append(((chip + 4 - step) % 4 * 2 + side, value))
    at_end = (chip == 0) | (chip == 3)
    owner = jnp.where(at_end, 3 - chip, chip)
    found.append((owner * 2 + core, jnp.where(at_end, ends, piece)))
    found.append((owner * 2 + 1 - core, jnp.where(at_end, ends_there, own_there)))
    return found


def pick_kernel(first_ref, second_ref, *refs):
    for axis in range(AXES):
        for plane in range(2):
            refs[AXES + axis * 2 + plane][...] = refs[axis][:, plane]


def pick_blocks(stored, tables, step, part):
    count = tables[0].shape[0]
    _, two, block_size, _ = stored.shape
    return pl.pallas_call(
        pick_kernel,
        grid_spec=pltpu.PrefetchScalarGridSpec(
            num_scalar_prefetch=AXES,
            grid=(count,),
            in_specs=[
                pl.BlockSpec(
                    (1, two, block_size, part), lambda i, *t, axis=axis: (t[axis][i], 0, 0, step * AXES + axis)
                )
                for axis in range(AXES)
            ],
            out_specs=[pl.BlockSpec((1, block_size, part), lambda i, *t: (i, 0, 0))] * (2 * AXES),
        ),
        out_shape=[jax.ShapeDtypeStruct((count, block_size, part), stored.dtype)] * (2 * AXES),
        cost_estimate=pl.CostEstimate(
            flops=0, transcendentals=0, bytes_accessed=count * two * block_size * part * 4 * AXES
        ),
        name="pick",
    )(*tables, *[stored] * AXES)


def scores_of(query, keys, present):
    scores = lax.dot_general(
        query, keys, (((1,), (1,)), ((), ())), preferred_element_type=jnp.float32
    ) * HEAD_DIM ** (-0.5)
    return jnp.where(present, scores, ABSENT)


def head_columns(head):
    return slice(head * HEAD_DIM, (head + 1) * HEAD_DIM)


def span_units(index_refs, query_refs, here_ref, far_refs, spans, span, first, together):
    per_step = query_refs[0].shape[0] // span
    part = query_refs[0].shape[1]
    units = []
    for local in (first + number for number in range(together)):
        in_group = pl.program_id(1) * per_step + local
        entry = pl.program_id(0) * spans + in_group
        rows = pl.ds(pl.multiple_of(local * span, span), span)
        for axis in range(AXES):
            here_at, far_at = index_refs[axis * 2][entry], index_refs[axis * 2 + 1][entry]
            here_block, far_block = jnp.maximum(here_at, 0), jnp.maximum(far_at, 0)
            for head in range(part // HEAD_DIM):
                columns = head_columns(head)
                here_columns = head_columns(axis * (part // HEAD_DIM) + head)
                query = query_refs[axis][rows, columns]
                here = scores_of(query, here_ref[here_block, 0, :, here_columns], here_at >= 0)
                far = scores_of(query, far_refs[axis][far_block, :, columns], far_at >= 0)
                lane = (in_group * (part // HEAD_DIM) + head) * 2
                units.append((axis, rows, columns, here_block, here_columns, far_block, lane, here, far))
    return units


def stats_kernel(spans, span, together, *refs):
    index_refs, refs = refs[:2 * AXES], refs[2 * AXES:]
    query_refs, here_ref, far_refs, out_refs = refs[:AXES], refs[AXES], refs[AXES + 1:2 * AXES + 1], refs[2 * AXES + 1:]
    turns = query_refs[0].shape[0] // span // together

    @pl.when(pl.program_id(1) == 0)
    def _():
        for out_ref in out_refs:
            out_ref[...] = jnp.zeros_like(out_ref)

    lanes = lax.broadcasted_iota(jnp.int32, out_refs[0].shape[1:], 1)

    def some(turn, carry):
        units = span_units(index_refs, query_refs, here_ref, far_refs, spans, span, turn * together, together)
        tops = [jnp.max(jnp.maximum(unit[-2], unit[-1]), axis=-1, keepdims=True) for unit in units]
        totals = [
            jnp.sum(jnp.exp(unit[-2] - top) + jnp.exp(unit[-1] - top), axis=-1, keepdims=True)
            for unit, top in zip(units, tops)
        ]
        for axis in range(AXES):
            kept = out_refs[axis][0]
            for unit, top, total in zip(units, tops, totals):
                if unit[0] == axis:
                    kept = jnp.where(lanes == unit[6], top, kept)
                    kept = jnp.where(lanes == unit[6] + 1, total, kept)
            out_refs[axis][0] = kept
        return carry

    lax.fori_loop(0, turns, some, 0)


def mix_kernel(spans, span, together, *refs):
    index_refs, refs = refs[:2 * AXES], refs[2 * AXES:]
    query_refs, here_ref, refs = refs[:AXES], refs[AXES], refs[AXES + 1:]
    far_refs, value_refs, mine_refs, their_refs, keep_refs, send_refs = (
        refs[i * AXES:(i + 1) * AXES] for i in range(6)
    )
    turns = query_refs[0].shape[0] // span // together
    lanes = lax.broadcasted_iota(jnp.int32, mine_refs[0].shape[1:], 1)

    def column(stats, at):
        return jnp.sum(jnp.where(lanes == at, stats, 0.0), axis=-1, keepdims=True)

    def some(out_refs, turn, carry):
        units = span_units(index_refs, query_refs, here_ref, far_refs, spans, span, turn * together, together)
        scales = []
        for unit in units:
            mine, theirs, at = mine_refs[unit[0]][0], their_refs[unit[0]][0], unit[6]
            my_top, their_top = column(mine, at), column(theirs, at)
            top = jnp.maximum(my_top, their_top)
            total = column(mine, at + 1) * jnp.exp(my_top - top) + column(theirs, at + 1) * jnp.exp(their_top - top)
            scales.append((top, 1.0 / total))
        weights = [
            jnp.concatenate(
                [jnp.exp(unit[-2] - top) * scale, jnp.exp(unit[-1] - top) * scale], axis=1
            ).astype(jnp.bfloat16)
            for unit, (top, scale) in zip(units, scales)
        ]
        for (axis, rows, columns, here_block, here_columns, far_block, _, _, _), weight in zip(units, weights):
            values = jnp.concatenate(
                [here_ref[here_block, 1, :, here_columns], value_refs[axis][far_block, :, columns]], axis=0
            )
            out_refs[axis][rows, columns] = jnp.dot(weight, values, preferred_element_type=jnp.float32)
        return carry

    for group, out_refs in enumerate((keep_refs, send_refs)):
        @pl.when(pl.program_id(0) == group)
        def _(out_refs=out_refs):
            lax.fori_loop(0, turns, functools.partial(some, out_refs), 0)


def span_call(kernel, indices, queries, stored, received, stats, step, part, spans, planes):
    rows = queries[0].shape[0] // 2
    span = rows // spans
    count, _, block_size, _ = stored.shape
    slots = received[0].shape[0]
    per_step = 8 if spans % 8 == 0 else spans
    steps = spans // per_step
    together = 2 if per_step % 2 == 0 else 1
    step_rows = per_step * span

    in_specs = [pl.BlockSpec((step_rows, part), lambda c, i, *t: (c * steps + i, 0))] * AXES
    in_specs += [pl.BlockSpec((count, planes, block_size, AXES * part), lambda c, i, *t: (0, 0, 0, step))]
    in_specs += [pl.BlockSpec((slots, block_size, part), lambda c, i, *t: (0, 0, 0))] * (planes * AXES)
    if stats:
        in_specs += [pl.BlockSpec((1, span, LANES), lambda c, i, *t: (c, 0, 0))] * AXES
        in_specs += [pl.BlockSpec((1, span, LANES), lambda c, i, *t: (1 - c, 0, 0))] * AXES
        out_specs = [pl.BlockSpec((step_rows, part), lambda c, i, *t: (jnp.where(c == 0, i, steps - 1), 0))] * AXES
        out_specs += [pl.BlockSpec((step_rows, part), lambda c, i, *t: (jnp.where(c == 0, 0, i), 0))] * AXES
        out_shape = [jax.ShapeDtypeStruct((rows, part), jnp.float32)] * (2 * AXES)
    else:
        out_specs = [pl.BlockSpec((1, span, LANES), lambda c, i, *t: (c, 0, 0))] * AXES
        out_shape = [jax.ShapeDtypeStruct((2, span, LANES), jnp.float32)] * AXES
    return pl.pallas_call(
        functools.partial(kernel, spans, span, together),
        grid_spec=pltpu.PrefetchScalarGridSpec(
            num_scalar_prefetch=2 * AXES,
            grid=(2, steps),
            in_specs=in_specs,
            out_specs=out_specs,
        ),
        out_shape=out_shape,
        cost_estimate=pl.CostEstimate(
            flops=8 * rows * NEIGH * block_size * part * AXES * planes,
            transcendentals=2 * rows * NEIGH * block_size * part * AXES // HEAD_DIM,
            bytes_accessed=(count + slots) * planes * block_size * part * 2 * AXES,
        ),
        name="mix" if stats else "stats",
    )(*indices, *queries, stored, *received, *stats)


def exchange_tables(neighbor_shard, neighbor_block, capacity):
    me = lax.axis_index("dp")
    both = jnp.concatenate([neighbor_shard, neighbor_block], axis=1)
    groups = jnp.stack([both] + [over_dp(both, bit) for bit in (1, 2, 3)])
    spans = both.shape[0]
    owners = groups[:, :, :NEIGH].reshape(4, spans * NEIGH)
    wanted = groups[:, :, NEIGH:].reshape(4, spans * NEIGH)
    order = jnp.arange(spans * NEIGH, dtype=jnp.int32)
    same = (owners[:, :, None] == owners[:, None, :]) & (order[None, None, :] < order[None, :, None])
    rank = jnp.sum(same.astype(jnp.int32), axis=2)
    slots = jnp.arange(capacity, dtype=jnp.int32)
    hit = (owners == me)[:, :, None] & (rank[:, :, None] == slots[None, None, :])
    table = jnp.sum(jnp.where(hit, wanted[:, :, None], 0), axis=1)
    sends, places = [], []
    for axis in range(AXES):
        near = 1 << axis
        partner = 3 ^ near
        sends.append(jnp.concatenate([table[near], table[3]]))
        here, far = [], []
        for position, group in enumerate((0, partner)):
            mine = (owners[group] == me).reshape(spans, NEIGH)
            other = (owners[group] == me ^ near).reshape(spans, NEIGH)
            block = wanted[group].reshape(spans, NEIGH)
            slot = rank[group].reshape(spans, NEIGH) + position * capacity
            here.append(jnp.max(jnp.where(mine, block, -1), axis=1))
            far.append(jnp.max(jnp.where(other, slot, -1), axis=1))
        places += [jnp.concatenate(here), jnp.concatenate(far)]
    return sends, places


def after(values, marker):
    return lax.optimization_barrier((values, marker))[0]


def work(tokens, w_query, w_output, neighbor_shard, neighbor_block, kv_store):
    local_width = w_query.shape[1]
    row_count, width = tokens.shape
    peers = lax.axis_size("dp")
    members = lax.axis_size("fsdp")
    passes = 2 if local_width % (2 * AXES * HEAD_DIM) == 0 else 1
    part = local_width // (passes * AXES)
    share = local_width // passes
    span_count = neighbor_shard.shape[0]
    capacity = max(2, 3 * span_count * NEIGH // (2 * peers))

    sends, places = exchange_tables(neighbor_shard, neighbor_block, capacity)
    stored = kv_store[0]
    picked = []
    for step in range(passes):
        picked.append(pick_blocks(stored, sends, step, part))

    def query_columns(step):
        columns = w_query[:, step * share:(step + 1) * share]
        if step > 0:
            columns = after(columns, picked[0])
        return lax.all_gather(columns, "dp", axis=0, tiled=True)

    def send_blocks(step, plane, marker):
        blocks = [picked[step][axis * 2 + plane] for axis in range(AXES)]
        if marker is not None:
            blocks = after(blocks, marker)
        return [over_dp(blocks[axis], 1 << axis) for axis in range(AXES)]

    pieces = pieces_over_fsdp(tokens)
    gathered = jnp.zeros((row_count, members * width), tokens.dtype)
    for owner, piece in pieces:
        gathered = lax.dynamic_update_slice(gathered, piece, (0, owner * width))
    normed = normalize(gathered)

    columns = [query_columns(step) for step in range(passes)]
    received = [[send_blocks(0, plane, None) for plane in range(2)]]
    asked, own_queries = [], []
    for step in range(passes):
        queries = jnp.dot(normed, columns[step], preferred_element_type=jnp.float32).astype(jnp.bfloat16)
        own_queries.append(queries)
        parts = [queries[:, axis * part:(axis + 1) * part] for axis in range(AXES)]
        asked.append([
            jnp.concatenate([parts[axis], over_dp(parts[axis], 3 ^ (1 << axis))], axis=0) for axis in range(AXES)
        ])
        if step > 0:
            received.append([send_blocks(step, 0, own_queries[0]), send_blocks(step, 1, queries)])

    attended = gathered
    if width != local_width:
        attended = jnp.zeros((row_count, members * local_width), jnp.bfloat16)
    for step in range(passes):
        common = dict(step=step, part=part, spans=span_count)
        mine = span_call(
            stats_kernel, places, asked[step], stored, received[step][0], [], planes=1, **common
        )
        if step == passes - 1:
            output_columns = lax.all_gather(after(w_output, mine), "dp", axis=0, tiled=True)
        theirs = [over_dp(mine[axis], 3 ^ (1 << axis)) for axis in range(AXES)]
        partial = span_call(
            mix_kernel, places, asked[step], stored, received[step][0] + received[step][1], list(mine) + theirs,
            planes=2, **common
        )
        others = [over_dp(partial[AXES + axis], 3 ^ (1 << axis)) for axis in range(AXES)]
        mixed = jnp.concatenate(
            [(partial[axis] + others[axis]).astype(jnp.bfloat16) for axis in range(AXES)], axis=1
        )
        mixed = lax.optimization_barrier(mixed)
        pieces = pieces_over_fsdp(mixed)
        for owner, piece in pieces:
            start = owner * local_width + step * share
            attended = lax.dynamic_update_slice(attended, piece, (0, start))
    summed = jnp.dot(attended, output_columns, preferred_element_type=jnp.float32)
    return summed.astype(jnp.bfloat16)


def solution(mesh):
    in_specs = (
        P("dp", "fsdp"),
        P("dp", "fsdp"),
        P("dp", "fsdp"),
        P("dp", None),
        P("dp", None),
        P("dp", None, None, None, "fsdp"),
    )
    out_specs = P("dp", "fsdp")
    return jax.shard_map(work, mesh=mesh, in_specs=in_specs, out_specs=out_specs, check_vma=False)
```
